32 devices in a mesh: inner: 4 (over x, core), outer: 8 (over z, y).
Axes of the slice: x: 2, y: 2, z: 4, core: 2. Of those that a mesh axis runs over, the one named last changes fastest.
Arguments:
- queries: bfloat16 [4096, 1024], P(('inner', 'outer')), may hold values from -6 to 6
- keys: bfloat16 [4096, 128], P(('inner', 'outer')), may hold values from -6 to 6
- values: bfloat16 [4096, 128], P(('inner', 'outer')), may hold values from -6 to 6
- out_grad: bfloat16 [4096, 1024], P(('inner', 'outer')), may hold values from -6 to 6
- forward_out: bfloat16 [4096, 1024], P(('inner', 'outer')), may hold values from -0.796875 to 0.796875
- log_sum_exp: float32 [8, 4096], P(None, ('inner', 'outer')), may hold values from 3 to 5
- span_table: int32 [64], replicated, may hold values from 0 to 63, each once
- mask_codes: int32 [32, 6], P(('inner', 'outer')), may hold values from 0 to 2
Outputs:
- query_grad: bfloat16 [4096, 1024], P(('inner', 'outer'))
- key_grad: bfloat16 [4096, 128], P(('inner', 'outer'))
- value_grad: bfloat16 [4096, 128], P(('inner', 'outer'))
The draws below stay inside these ranges and needn't reach their ends.
Inputs may be any that keep to these rules, and one draw needn't show every extreme that they name: `span_table`: each span number appears exactly once.
All inputs are finite; a program needn't handle non-finite values.
Results may differ from the reference program's by a relative error of at most 0.0057.
Values may be sent and summed in bfloat16 or wider, within the bound.
A program may use at most 64 MiB of HBM per device.

```python
import jax
import jax.numpy as jnp
from jax import lax

H = 8
DH = 128
ROWS = 128
REMOTE = 6
BLOCKS = 32
TOKENS = 4096
SPANS = 64
N_INNER = 4
N_OUTER = 8


def place_ends(result, rng, smallest, largest):
    spot = [jax.random.randint(jax.random.fold_in(rng, axis), (), 0, length) for axis, length in enumerate(result.shape)]
    widest = result.shape.index(max(result.shape))
    beside = spot[:widest] + [(spot[widest] + 1) % result.shape[widest]] + spot[widest + 1:]
    return result.at[tuple(spot)].set(smallest).at[tuple(beside)].set(largest)


def level_of(rng, extent, split, low, largest):
    factor_of, own = 1.0, jax.random.fold_in(rng, 6)
    for position, blocks in split:
        heights = jnp.exp(jax.random.uniform(jax.random.fold_in(own, position), (blocks,), jnp.float32, low / len(split), largest / len(split)))
        factor_of = factor_of * jnp.repeat(heights, extent[position] // blocks).reshape([-1 if axis == position else 1 for axis in range(len(extent))])
    return factor_of


def gaussian(stream_key, dims, deviation, reach, split=(), kind=jnp.bfloat16):
    values = deviation * jax.random.normal(stream_key, dims, jnp.float32)
    if split:
        values = values * level_of(stream_key, dims, split, -0.22, 0.18)
    return jnp.clip(values, -reach, reach).astype(kind)


def setup_inputs(seed: int = 0) -> dict:
    arg_keys = jax.random.split(jax.random.key(seed), 9)
    queries = gaussian(arg_keys[0], (TOKENS, H * DH), 1.0, 6.0, ((0, 32),))
    keys = gaussian(arg_keys[1], (TOKENS, DH), 1.0, 6.0, ((0, 32),))
    values = gaussian(arg_keys[2], (TOKENS, DH), 1.0, 6.0, ((0, 32),))
    out_grad = gaussian(arg_keys[3], (TOKENS, H * DH), 1.0, 6.0, ((0, 32),))
    forward_out = gaussian(arg_keys[4], (TOKENS, H * DH), 0.1, 0.796875, ((0, 32),))
    log_sum_exp = jnp.clip(3.0 + 2.0 * jax.random.uniform(arg_keys[5], (H, TOKENS), jnp.float32) ** level_of(arg_keys[5], (H, TOKENS), ((1, 32),), -0.2, 0.2), 3.0, 5.0)
    span_table = jax.random.permutation(arg_keys[6], SPANS).astype(jnp.int32)
    mask_codes = place_ends(jax.random.randint(arg_keys[7], (BLOCKS, REMOTE), 0, 3), jax.random.fold_in(arg_keys[7], 1), 0, 2).astype(jnp.int32)
    return dict(queries=queries, keys=keys, values=values, out_grad=out_grad, forward_out=forward_out, log_sum_exp=log_sum_exp, span_table=span_table, mask_codes=mask_codes)


WINDOW_PATH = ((0, 0), (1, 0), (2, 0), (2, 1), (3, 1), (4, 1), (4, 2))


def block_terms(queries, grads_out, log_sum_exp, delta, query_pos, key_block, value_block, key_pos, mask_code):
    head_width = key_block.shape[-1]
    score_scale = head_width ** -0.5
    row_count = queries.shape[0]
    head_count = log_sum_exp.shape[0]
    query_heads = queries.astype(jnp.float32).reshape(row_count, head_count, head_width)
    gradient_heads = grads_out.astype(jnp.float32).reshape(row_count, head_count, head_width)
    key_float = key_block.astype(jnp.float32)
    value_float = value_block.astype(jnp.float32)
    scores = jnp.einsum("qhd,kd->hqk", query_heads, key_float) * score_scale
    allowed = (mask_code == 2) | ((mask_code == 1) & (key_pos[None, :] <= query_pos[:, None]))
    probs = jnp.where(allowed[None], jnp.exp(scores - log_sum_exp[:, :, None]), 0.0)
    probs_low = lax.optimization_barrier(probs.astype(jnp.bfloat16)).astype(jnp.float32)
    value_part = jnp.einsum("hqk,qhd->kd", probs_low, gradient_heads)
    dprob = jnp.einsum("qhd,kd->hqk", gradient_heads, value_float)
    dscore = (probs * (dprob - delta[:, :, None])) * score_scale
    dscore_low = lax.optimization_barrier(dscore.astype(jnp.bfloat16)).astype(jnp.float32)
    query_part = jnp.einsum("hqk,kd->qhd", dscore_low, key_float).reshape(row_count, head_count * head_width)
    key_part = jnp.einsum("hqk,qhd->kd", dscore_low, query_heads)
    return query_part, key_part, value_part


def reference(queries, keys, values, out_grad, forward_out, log_sum_exp, span_table, mask_codes):
    inner_count = N_INNER
    outer_count = N_OUTER
    half_rows = ROWS // 2

    def by_device(array):
        return array.reshape((inner_count, outer_count, ROWS) + array.shape[1:])

    query_dev = by_device(queries)
    key_dev = by_device(keys)
    value_dev = by_device(values)
    grad_dev = by_device(out_grad)
    delta_rows = jnp.sum((out_grad.astype(jnp.float32) * forward_out.astype(jnp.float32)).reshape(TOKENS, H, DH), axis=2)
    delta_dev = by_device(delta_rows).transpose(0, 1, 3, 2)
    lse_dev = log_sum_exp.reshape(H, inner_count, outer_count, ROWS).transpose(1, 2, 0, 3)
    span_pairs = span_table.reshape(inner_count, outer_count, 2)
    offsets = jnp.arange(half_rows, dtype=jnp.int32)
    positions = (span_pairs[:, :, :, None] * half_rows + offsets).reshape(inner_count, outer_count, ROWS).astype(jnp.int32)
    codes_dev = mask_codes.reshape(inner_count, outer_count, REMOTE)

    def one_slice(inner_at):
        query_here = query_dev[inner_at]
        grad_here = grad_dev[inner_at]
        lse_here = lse_dev[inner_at]
        delta_here = delta_dev[inner_at]
        pos_here = positions[inner_at]
        query_sum = jnp.zeros((outer_count, ROWS, H * DH), jnp.float32)
        key_parts = []
        value_parts = []
        for window_step, (inner_back, outer_back) in enumerate(WINDOW_PATH):
            source = (inner_at - inner_back) % inner_count
            key_seen = jnp.roll(key_dev[source], outer_back, axis=0)
            value_seen = jnp.roll(value_dev[source], outer_back, axis=0)
            pos_seen = jnp.roll(positions[source], outer_back, axis=0)
            if window_step == 0:
                code_seen = jnp.ones((outer_count,), jnp.int32)
            else:
                code_seen = codes_dev[inner_at, :, window_step - 1]
            query_part, key_part, value_part = jax.vmap(block_terms)(
                query_here, grad_here, lse_here, delta_here, pos_here, key_seen, value_seen, pos_seen, code_seen)
            query_sum = query_sum + query_part
            key_parts.append(key_part)
            value_parts.append(value_part)
        return query_sum.astype(jnp.bfloat16), jnp.stack(key_parts), jnp.stack(value_parts)

    query_total, key_parts, value_parts = lax.map(one_slice, jnp.arange(inner_count, dtype=jnp.int32))
    key_total = jnp.zeros((inner_count, outer_count, ROWS, DH), jnp.float32)
    value_total = jnp.zeros((inner_count, outer_count, ROWS, DH), jnp.float32)
    for window_step, (inner_back, outer_back) in enumerate(WINDOW_PATH):
        key_total = key_total + jnp.roll(key_parts[:, window_step], (-inner_back, -outer_back), axis=(0, 1))
        value_total = value_total + jnp.roll(value_parts[:, window_step], (-inner_back, -outer_back), axis=(0, 1))
    return (query_total.reshape(TOKENS, H * DH),
            key_total.reshape(TOKENS, DH).astype(jnp.bfloat16),
            value_total.reshape(TOKENS, DH).astype(jnp.bfloat16))
```

```python
import functools

import jax
import jax.numpy as jnp
from jax import lax
from jax.experimental import pallas as pl
from jax.experimental.pallas import tpu as pltpu
from jax.sharding import PartitionSpec as P

WINDOW_PATH = ((0, 0), (1, 0), (2, 0), (2, 1), (3, 1), (4, 1), (4, 2))
STEP_ORDER = (1, 2, 6, 5, 4, 3)
SEND_ORDER = (3, 4, 6, 5, 2, 1)
MESH = pl.DeviceIdType.MESH


def kernel(inner_count, outer_count, q_hbm, k_hbm, v_hbm, do_hbm, o_hbm, lse_hbm, span_hbm, code_hbm,
           dq_ref, dk_ref, dv_ref,
           lse_ref, span_ref, code_ref, q_vm, do_vm, o_vm, kv_own, kv_in, g_out, g_in, dq_acc, own_acc,
           load_sem, kv_send, kv_recv, g_send, g_recv):
    inner_at = lax.axis_index("inner")
    outer_at = lax.axis_index("outer")
    head_count, rows, width = q_vm.shape
    half = rows // 2
    scale = width ** (-0.5)
    steps = range(1, len(WINDOW_PATH))

    def shifted(a, c):
        u = lax.rem(inner_at + a % inner_count, inner_count)
        w = lax.rem(outer_at + c % outer_count, outer_count)
        return u, w

    def device(step, sign):
        a, c = WINDOW_PATH[step]
        return shifted(sign * a, sign * c)

    barrier = pltpu.get_barrier_semaphore()
    for step in SEND_ORDER:
        pl.semaphore_signal(barrier, inc=1, device_id=device(step, -1), device_id_type=MESH)

    loads = []

    def load(src, dst, slot):
        copy = pltpu.make_async_copy(src, dst, load_sem.at[slot])
        copy.start()
        loads.append(copy)

    load(k_hbm, kv_own.at[0], 0)
    load(v_hbm, kv_own.at[1], 1)
    load(lse_hbm, lse_ref, 2 + 3 * head_count)
    load(span_hbm, span_ref, 3 + 3 * head_count)
    load(code_hbm, code_ref, 4 + 3 * head_count)
    for h in range(head_count):
        columns = pl.ds(h * width, width)
        load(q_hbm.at[:, columns], q_vm.at[h], 2 + 3 * h)
        load(do_hbm.at[:, columns], do_vm.at[h], 3 + 3 * h)
        load(o_hbm.at[:, columns], o_vm.at[h], 4 + 3 * h)
    for copy in loads[:2]:
        copy.wait()

    pl.semaphore_wait(barrier, len(steps))

    def kv_copy(step, part):
        return pltpu.make_async_remote_copy(
            src_ref=kv_own.at[part], dst_ref=kv_in.at[step - 1, part],
            send_sem=kv_send.at[step - 1, part], recv_sem=kv_recv.at[step - 1, part],
            device_id=device(step, 1), device_id_type=MESH)

    def g_copy(step, part):
        return pltpu.make_async_remote_copy(
            src_ref=g_out.at[step - 1, part], dst_ref=g_in.at[step - 1, part],
            send_sem=g_send.at[step - 1, part], recv_sem=g_recv.at[step - 1, part],
            device_id=device(step, -1), device_id_type=MESH)

    for step in SEND_ORDER:
        for part in range(2):
            kv_copy(step, part).start()
    for copy in loads[2:]:
        copy.wait()

    def spans(step):
        u, w = device(step, -1)
        block = u * outer_count + w
        return span_ref[2 * block], span_ref[2 * block + 1]

    def position(step, dim):
        first, second = spans(step)
        at = lax.broadcasted_iota(jnp.int32, (rows, rows), dim)
        return jnp.where(at < half, first * half + at, second * half + at - half)

    query_pos = position(0, 1)
    lse_row = jnp.concatenate([lse_ref[h:h + 1, :] for h in range(head_count)], axis=1)
    delta_rows = []
    for h in range(head_count):
        product = do_vm[h].astype(jnp.float32) * o_vm[h].astype(jnp.float32)
        delta_rows.append(jnp.sum(product.T, axis=0, keepdims=True))
    delta_row = jnp.concatenate(delta_rows, axis=1)
    features = head_count * rows

    def dot(x, y, dims):
        return lax.dot_general(x, y, (dims, ((), ())), preferred_element_type=jnp.float32)

    def visit(step, key_block, value_block):
        q_all = q_vm[...].reshape(features, width)
        do_all = do_vm[...].reshape(features, width)
        if step == 0:
            allowed = position(0, 0) <= query_pos
        else:
            code = code_ref[0, step - 1]
            limit = jnp.where(code == 2, jnp.int32(2 ** 31 - 1), jnp.int32(-1))
            reach = jnp.where(code == 1, query_pos, limit)
            allowed = position(step, 0) <= reach
        allowed = jnp.concatenate([allowed] * head_count, axis=1)
        scores = dot(key_block, q_all, ((1,), (1,))) * scale
        probs = jnp.where(allowed, jnp.exp(scores - lse_row), 0.0)
        dprob = dot(value_block, do_all, ((1,), (1,)))
        dscore = (probs * (dprob - delta_row) * scale).astype(jnp.bfloat16)
        value_part = dot(probs.astype(jnp.bfloat16), do_all, ((1,), (0,)))
        key_part = dot(dscore, q_all, ((1,), (0,)))
        query_part = dot(key_block.T, dscore, ((1,), (0,)))
        return query_part, key_part, value_part

    dq_acc[...], own_acc[0], own_acc[1] = visit(0, kv_own[0], kv_own[1])
    def put(step, part, value):
        g_out[step - 1, part] = value.astype(jnp.bfloat16)
        g_copy(step, part).start()

    for step in STEP_ORDER:
        for part in range(2):
            kv_copy(step, part).wait_recv()
        query_part, key_part, value_part = visit(step, kv_in[step - 1, 0], kv_in[step - 1, 1])
        put(step, 1, value_part)
        put(step, 0, key_part)
        dq_acc[...] += query_part
    for h in range(head_count):
        columns = pl.ds(h * rows, rows)
        dq_ref[:, pl.ds(h * width, width)] = dq_acc[:, columns].T.astype(jnp.bfloat16)
    for part, out in ((1, dv_ref), (0, dk_ref)):
        total = own_acc[part]
        for step in STEP_ORDER:
            g_copy(step, part).wait_recv()
            total = total + g_in[step - 1, part].astype(jnp.float32)
        out[...] = total.astype(jnp.bfloat16)
    for step in STEP_ORDER:
        for part in range(2):
            kv_copy(step, part).wait_send()
            g_copy(step, part).wait_send()


def finish(dq_in, dk_in, dv_in, dq_out, dk_out, dv_out, sems):
    moves = [pltpu.make_async_copy(src, dst, sems.at[slot])
             for slot, (src, dst) in enumerate(((dq_in, dq_out), (dk_in, dk_out), (dv_in, dv_out)))]
    for move in moves:
        move.start()
    for move in moves:
        move.wait()


def shards(queries, keys, values, out_grad, forward_out, log_sum_exp, span_table, mask_codes):
    rows, features = queries.shape
    width = keys.shape[1]
    heads = log_sum_exp.shape[0]
    remote = len(WINDOW_PATH) - 1
    hbm = pl.BlockSpec(memory_space=pl.ANY)
    vmem = pl.BlockSpec(memory_space=pltpu.VMEM)
    grads = (
        jax.ShapeDtypeStruct((rows, features), jnp.bfloat16),
        jax.ShapeDtypeStruct((rows, width), jnp.bfloat16),
        jax.ShapeDtypeStruct((rows, width), jnp.bfloat16),
    )
    parts = pl.pallas_call(
        functools.partial(kernel, lax.axis_size("inner"), lax.axis_size("outer")),
        out_shape=grads,
        in_specs=[hbm] * 8,
        out_specs=(vmem, vmem, vmem),
        scratch_shapes=[
            pltpu.VMEM((heads, rows), jnp.float32),
            pltpu.SMEM(span_table.shape, jnp.int32),
            pltpu.SMEM(mask_codes.shape, jnp.int32),
            pltpu.VMEM((heads, rows, width), jnp.bfloat16),
            pltpu.VMEM((heads, rows, width), jnp.bfloat16),
            pltpu.VMEM((heads, rows, width), jnp.bfloat16),
            pltpu.VMEM((2, rows, width), jnp.bfloat16),
            pltpu.VMEM((remote, 2, rows, width), jnp.bfloat16),
            pltpu.VMEM((remote, 2, rows, width), jnp.bfloat16),
            pltpu.VMEM((remote, 2, rows, width), jnp.bfloat16),
            pltpu.VMEM((width, heads * rows), jnp.float32),
            pltpu.VMEM((2, rows, width), jnp.float32),
            pltpu.SemaphoreType.DMA((5 + 3 * heads,)),
            pltpu.SemaphoreType.DMA((remote, 2)),
            pltpu.SemaphoreType.DMA((remote, 2)),
            pltpu.SemaphoreType.DMA((remote, 2)),
            pltpu.SemaphoreType.DMA((remote, 2)),
        ],
        compiler_params=pltpu.CompilerParams(
            collective_id=0, has_side_effects=True, vmem_limit_bytes=16 * 2 ** 20),
    )(*(pltpu.with_memory_space_constraint(x, pltpu.HBM) for x in (queries, keys, values, out_grad, forward_out, log_sum_exp, span_table, mask_codes)))
    return pl.pallas_call(
        finish,
        out_shape=grads,
        in_specs=[hbm] * 3,
        out_specs=(hbm, hbm, hbm),
        scratch_shapes=[pltpu.SemaphoreType.DMA((3,))],
        compiler_params=pltpu.CompilerParams(vmem_limit_bytes=2 ** 20),
    )(*parts)


def solution(mesh):
    return jax.shard_map(
        shards,
        mesh=mesh,
        in_specs=(
            P(("inner", "outer"), None),
            P(("inner", "outer"), None),
            P(("inner", "outer"), None),
            P(("inner", "outer"), None),
            P(("inner", "outer"), None),
            P(None, ("inner", "outer")),
            P(),
            P(("inner", "outer"), None),
        ),
        out_specs=(
            P(("inner", "outer"), None),
            P(("inner", "outer"), None),
            P(("inner", "outer"), None),
        ),
        check_vma=False,
    )
```

```python
import functools

import jax
import jax.numpy as jnp
from jax import lax
from jax.experimental import pallas as pl
from jax.experimental.pallas import tpu as pltpu
from jax.sharding import PartitionSpec as P

WINDOW_PATH = ((0, 0), (1, 0), (2, 0), (2, 1), (3, 1), (4, 1), (4, 2))
EVEN_ORDER = (2, 1, 3, 4, 5, 6)
ODD_ORDER = (1, 2, 4, 5, 3, 6)
MESH = pl.DeviceIdType.MESH


def kernel(inner_count, outer_count, q_hbm, k_hbm, v_hbm, do_hbm, o_hbm, lse_hbm, span_hbm, code_hbm,
           dq_ref, dk_ref, dv_ref,
           lse_ref, span_ref, code_ref, q_vm, do_vm, o_vm, kv_own, kv_in, g_out, g_in, mail, held, dq_acc, own_acc,
           load_sem, kv_send, kv_recv, relay_send, g_send, g_recv, mail_recv):
    inner_at = lax.axis_index("inner")
    outer_at = lax.axis_index("outer")
    odd = lax.rem(inner_at, 2)
    is_even, is_odd = odd == 0, odd == 1
    head_count, rows, width = q_vm.shape
    half = rows // 2
    scale = width ** (-0.5)

    def pick(even, other):
        return even if even == other else even + odd * (other - even)

    def shifted(a, c):
        return lax.rem(inner_at + a, inner_count), lax.rem(outer_at + c, outer_count)

    def later(step, other=None):
        a, c = WINDOW_PATH[step]
        d, e = WINDOW_PATH[step if other is None else other]
        return shifted(pick(a % inner_count, d % inner_count), pick(c % outer_count, e % outer_count))

    def earlier(step, other=None):
        a, c = WINDOW_PATH[step]
        d, e = WINDOW_PATH[step if other is None else other]
        return shifted(pick(-a % inner_count, -d % inner_count), pick(-c % outer_count, -e % outer_count))

    mate = (inner_at + 1 - 2 * odd, outer_at)

    barrier = pltpu.get_barrier_semaphore()

    def greet(device):
        pl.semaphore_signal(barrier, inc=1, device_id=device, device_id_type=MESH)

    for step in (5, 6, 2):
        greet(earlier(step))
    greet(mate)

    @pl.when(is_odd)
    def _():
        greet(earlier(4))
        greet(earlier(3))

    loads = []

    def load(src, dst, slot):
        copy = pltpu.make_async_copy(src, dst, load_sem.at[slot])
        copy.start()
        loads.append(copy)

    load(k_hbm, kv_own.at[0], 0)
    load(v_hbm, kv_own.at[1], 1)
    load(lse_hbm, lse_ref, 2 + 3 * head_count)
    load(span_hbm, span_ref, 3 + 3 * head_count)
    load(code_hbm, code_ref, 4 + 3 * head_count)
    for h in range(head_count):
        columns = pl.ds(h * width, width)
        load(q_hbm.at[:, columns], q_vm.at[h], 2 + 3 * h)
        load(do_hbm.at[:, columns], do_vm.at[h], 3 + 3 * h)
        load(o_hbm.at[:, columns], o_vm.at[h], 4 + 3 * h)
    for copy in loads[:2]:
        copy.wait()

    pl.semaphore_wait(barrier, 5)

    def remote(src, dst, send_sem, recv_sem, device):
        return pltpu.make_async_remote_copy(
            src_ref=src, dst_ref=dst, send_sem=send_sem, recv_sem=recv_sem,
            device_id=device, device_id_type=MESH)

    def kv_copy(slot, device):
        return remote(kv_own, kv_in.at[slot - 1], kv_send.at[slot - 1], kv_recv.at[slot - 1], device)

    def relay(source, slot):
        return remote(kv_in.at[source - 1], kv_in.at[slot - 1], relay_send.at[slot - 1], kv_recv.at[slot - 1], mate)

    kv_mate = kv_copy(1, mate)
    kv_sends = (kv_copy(pick(4, 3), later(4, 3)), kv_copy(5, later(5)), kv_copy(6, later(6)), kv_copy(2, later(2)))
    relays = {2: relay(2, 1), 4: relay(4, 3), 5: relay(5, 4)}

    def wait_kv(slot):
        kv_copy(slot, mate).wait_recv()

    @pl.when(is_even)
    def _():
        kv_sends[0].start()
        kv_sends[1].start()

    @pl.when(is_odd)
    def _():
        kv_sends[1].start()
        kv_sends[0].start()

    for copy in kv_sends[2:]:
        copy.start()

    @pl.when(is_even)
    def _():
        kv_mate.start()

    for copy in loads[2:]:
        copy.wait()

    def g_copy(source, slot, device):
        return remote(g_out.at[source - 1], g_in.at[slot - 1], g_send.at[source - 1], g_recv.at[slot - 1], device)

    def mail_copy(source, slot):
        return remote(g_out.at[source - 1], mail.at[slot - 2], g_send.at[source - 1], mail_recv.at[slot - 2], mate)

    def position(a, c, dim):
        u, w = shifted(a, c)
        block = u * outer_count + w
        first, second = span_ref[2 * block], span_ref[2 * block + 1]
        at = lax.broadcasted_iota(jnp.int32, (rows, rows), dim)
        return jnp.where(at < half, first * half + at, second * half + at - half)

    query_pos = position(0, 0, 1)
    lse_row = jnp.concatenate([lse_ref[h:h + 1, :] for h in range(head_count)], axis=1)
    delta_rows = []
    for h in range(head_count):
        product = do_vm[h].astype(jnp.float32) * o_vm[h].astype(jnp.float32)
        delta_rows.append(jnp.sum(product.T, axis=0, keepdims=True))
    delta_row = jnp.concatenate(delta_rows, axis=1)
    features = head_count * rows

    def dot(x, y, dims):
        return lax.dot_general(x, y, (dims, ((), ())), preferred_element_type=jnp.float32)

    def visit(even, other, key_block, value_block):
        q_all = q_vm[...].reshape(features, width)
        do_all = do_vm[...].reshape(features, width)
        if even == 0:
            allowed = position(0, 0, 0) <= query_pos
        else:
            (a, c), (d, e) = WINDOW_PATH[even], WINDOW_PATH[other]
            code = code_ref[0, pick(even, other) - 1]
            limit = jnp.where(code == 2, jnp.int32(2 ** 31 - 1), jnp.int32(-1))
            reach = jnp.where(code == 1, query_pos, limit)
            key_pos = position(pick(-a % inner_count, -d % inner_count), pick(-c % outer_count, -e % outer_count), 0)
            allowed = key_pos <= reach
        allowed = jnp.concatenate([allowed] * head_count, axis=1)
        scores = dot(key_block, q_all, ((1,), (1,))) * scale
        probs = jnp.where(allowed, jnp.exp(scores - lse_row), 0.0)
        dprob = dot(value_block, do_all, ((1,), (1,)))
        dscore = (probs * (dprob - delta_row) * scale).astype(jnp.bfloat16)
        value_part = dot(probs.astype(jnp.bfloat16), do_all, ((1,), (0,)))
        key_part = dot(dscore, q_all, ((1,), (0,)))
        query_part = dot(key_block.T, dscore, ((1,), (0,)))
        return query_part, key_part, value_part

    def step(at):
        even, other = EVEN_ORDER[at], ODD_ORDER[at]
        slot = pick(even, other)
        query_part, key_part, value_part = visit(even, other, kv_in[slot - 1, 0], kv_in[slot - 1, 1])
        dq_acc[...] += query_part
        return key_part, value_part

    def send_now(at, parts, device):
        even, other = EVEN_ORDER[at], ODD_ORDER[at]
        slot = pick(even, other)
        for part in range(2):
            g_out[slot - 1, part] = parts[part].astype(jnp.bfloat16)
        copy = g_copy(slot, slot, device)
        copy.start()
        return copy

    mails, sums = [], []

    def share(at, parts):
        source, slot = EVEN_ORDER[at], ODD_ORDER[at]
        copy = mail_copy(source, slot)
        mails.append(copy)

        @pl.when(is_even)
        def _():
            for part in range(2):
                g_out[source - 1, part] = parts[part].astype(jnp.bfloat16)
            copy.start()

        @pl.when(is_odd)
        def _():
            for part in range(2):
                held[slot - 2, part] = parts[part]

    def combine(slot):
        copy = g_copy(slot, slot, earlier(slot))
        sums.append(copy)

        @pl.when(is_odd)
        def _():
            mail_copy(slot, slot).wait_recv()
            for part in range(2):
                total = held[slot - 2, part] + mail[slot - 2, part].astype(jnp.float32)
                g_out[slot - 1, part] = total.astype(jnp.bfloat16)
            copy.start()

    dq_acc[...], own_acc[0], own_acc[1] = visit(0, 0, kv_own[0], kv_own[1])

    @pl.when(is_odd)
    def _():
        wait_kv(2)
        relays[2].start()

    wait_kv(pick(2, 1))
    back = shifted(pick(-2 % inner_count, -1 % inner_count), 0)
    sent = [send_now(0, step(0), back)]

    @pl.when(is_even)
    def _():
        wait_kv(1)

    share(1, step(1))

    @pl.when(is_odd)
    def _():
        wait_kv(4)
        relays[4].start()
        wait_kv(5)
        relays[5].start()

    @pl.when(is_even)
    def _():
        wait_kv(3)

    share(2, step(2))

    @pl.when(is_even)
    def _():
        wait_kv(4)

    share(3, step(3))
    combine(2)
    wait_kv(pick(5, 3))
    sent.append(send_now(4, step(4), earlier(5, 3)))
    combine(4)
    wait_kv(6)
    sent.append(send_now(5, step(5), earlier(6)))
    combine(5)

    for h in range(head_count):
        columns = pl.ds(h * rows, rows)
        dq_ref[:, pl.ds(h * width, width)] = dq_acc[:, columns].T.astype(jnp.bfloat16)

    @pl.when(is_even)
    def _():
        g_copy(1, 1, mate).wait_recv()
        for part in range(2):
            own_acc[part] += g_in[0, part].astype(jnp.float32)

    last = (2, 6, 5, pick(4, 3))
    for slot in last:
        g_copy(slot, slot, mate).wait_recv()
    for part, out in ((0, dk_ref), (1, dv_ref)):
        total = own_acc[part]
        for slot in last:
            total = total + g_in[slot - 1, part].astype(jnp.float32)
        out[...] = total.astype(jnp.bfloat16)

    for copy in kv_sends + tuple(sent):
        copy.wait_send()

    @pl.when(is_even)
    def _():
        for copy in [kv_mate] + mails:
            copy.wait_send()

    @pl.when(is_odd)
    def _():
        for copy in list(relays.values()) + sums:
            copy.wait_send()


def finish(dq_in, dk_in, dv_in, dq_out, dk_out, dv_out, sems):
    moves = [pltpu.make_async_copy(src, dst, sems.at[slot])
             for slot, (src, dst) in enumerate(((dq_in, dq_out), (dk_in, dk_out), (dv_in, dv_out)))]
    for move in moves:
        move.start()
    for move in moves:
        move.wait()


def shards(queries, keys, values, out_grad, forward_out, log_sum_exp, span_table, mask_codes):
    rows, features = queries.shape
    width = keys.shape[1]
    heads = log_sum_exp.shape[0]
    remote = len(WINDOW_PATH) - 1
    hbm = pl.BlockSpec(memory_space=pl.ANY)
    vmem = pl.BlockSpec(memory_space=pltpu.VMEM)
    grads = (
        jax.ShapeDtypeStruct((rows, features), jnp.bfloat16),
        jax.ShapeDtypeStruct((rows, width), jnp.bfloat16),
        jax.ShapeDtypeStruct((rows, width), jnp.bfloat16),
    )
    parts = pl.pallas_call(
        functools.partial(kernel, lax.axis_size("inner"), lax.axis_size("outer")),
        out_shape=grads,
        in_specs=[hbm] * 8,
        out_specs=(vmem, vmem, vmem),
        scratch_shapes=[
            pltpu.VMEM((heads, rows), jnp.float32),
            pltpu.SMEM(span_table.shape, jnp.int32),
            pltpu.SMEM(mask_codes.shape, jnp.int32),
            pltpu.VMEM((heads, rows, width), jnp.bfloat16),
            pltpu.VMEM((heads, rows, width), jnp.bfloat16),
            pltpu.VMEM((heads, rows, width), jnp.bfloat16),
            pltpu.VMEM((2, rows, width), jnp.bfloat16),
            pltpu.VMEM((remote, 2, rows, width), jnp.bfloat16),
            pltpu.VMEM((remote, 2, rows, width), jnp.bfloat16),
            pltpu.VMEM((remote, 2, rows, width), jnp.bfloat16),
            pltpu.VMEM((4, 2, rows, width), jnp.bfloat16),
            pltpu.VMEM((4, 2, rows, width), jnp.float32),
            pltpu.VMEM((width, heads * rows), jnp.float32),
            pltpu.VMEM((2, rows, width), jnp.float32),
            pltpu.SemaphoreType.DMA((5 + 3 * heads,)),
            pltpu.SemaphoreType.DMA((remote,)),
            pltpu.SemaphoreType.DMA((remote,)),
            pltpu.SemaphoreType.DMA((remote,)),
            pltpu.SemaphoreType.DMA((remote,)),
            pltpu.SemaphoreType.DMA((remote,)),
            pltpu.SemaphoreType.DMA((4,)),
        ],
        compiler_params=pltpu.CompilerParams(
            collective_id=0, has_side_effects=True, vmem_limit_bytes=16 * 2 ** 20),
    )(*(pltpu.with_memory_space_constraint(x, pltpu.HBM) for x in (queries, keys, values, out_grad, forward_out, log_sum_exp, span_table, mask_codes)))
    return pl.pallas_call(
        finish,
        out_shape=grads,
        in_specs=[hbm] * 3,
        out_specs=(hbm, hbm, hbm),
        scratch_shapes=[pltpu.SemaphoreType.DMA((3,))],
        compiler_params=pltpu.CompilerParams(vmem_limit_bytes=2 ** 20),
    )(*parts)


def solution(mesh):
    return jax.shard_map(
        shards,
        mesh=mesh,
        in_specs=(
            P(("inner", "outer"), None),
            P(("inner", "outer"), None),
            P(("inner", "outer"), None),
            P(("inner", "outer"), None),
            P(("inner", "outer"), None),
            P(None, ("inner", "outer")),
            P(),
            P(("inner", "outer"), None),
        ),
        out_specs=(
            P(("inner", "outer"), None),
            P(("inner", "outer"), None),
            P(("inner", "outer"), None),
        ),
        check_vma=False,
    )
```

```python
import functools

import jax
import jax.numpy as jnp
from jax import lax
from jax.experimental import pallas as pl
from jax.experimental.pallas import tpu as pltpu
from jax.sharding import PartitionSpec as P

WINDOW_PATH = ((0, 0), (1, 0), (2, 0), (2, 1), (3, 1), (4, 1), (4, 2))
MESH = pl.DeviceIdType.MESH


def kernel(inner_count, outer_count, q_hbm, k_hbm, v_hbm, do_hbm, o_hbm, lse_hbm, span_hbm, code_hbm,
           dq_ref, dk_ref, dv_ref,
           lse_ref, span_ref, code_ref, q_vm, do_vm, o_vm, meta, kv, g_out, g_in, held, dq_acc, dq_out, dq_in, own_acc,
           load_sem, kv_send, kv_recv, g_send, g_recv, pair_send, pair_recv):
    inner_at = lax.axis_index("inner")
    outer_at = lax.axis_index("outer")
    odd = lax.rem(inner_at, 2)
    is_even, is_odd = odd == 0, odd == 1
    _, head_count, rows, width = q_vm.shape
    half = rows // 2
    scale = width ** (-0.5)
    steps = len(WINDOW_PATH)
    first_code = 2 * head_count

    def pick(even, other):
        return even if even == other else even + odd * (other - even)

    def shifted(a, c):
        return lax.rem(inner_at + a, inner_count), lax.rem(outer_at + c, outer_count)

    def later(step, other=None):
        a, c = WINDOW_PATH[step]
        d, e = WINDOW_PATH[step if other is None else other]
        return shifted(pick(a % inner_count, d % inner_count), pick(c % outer_count, e % outer_count))

    def earlier(step, other=None):
        a, c = WINDOW_PATH[step]
        d, e = WINDOW_PATH[step if other is None else other]
        return shifted(pick(-a % inner_count, -d % inner_count), pick(-c % outer_count, -e % outer_count))

    mate = (inner_at + 1 - 2 * odd, outer_at)

    barrier = pltpu.get_barrier_semaphore()

    def greet(device):
        pl.semaphore_signal(barrier, inc=1, device_id=device, device_id_type=MESH)

    for step in (5, 6, 2):
        greet(earlier(step))

    @pl.when(is_odd)
    def _():
        greet(earlier(4))
        greet(earlier(3))

    greet(mate)
    loads = []

    def load(src, dst, slot):
        copy = pltpu.make_async_copy(src, dst, load_sem.at[slot])
        copy.start()
        loads.append(copy)

    load(k_hbm, kv.at[0, 0], 0)
    load(v_hbm, kv.at[0, 1], 1)
    load(lse_hbm, lse_ref, 2 + 3 * head_count)
    load(span_hbm, span_ref, 3 + 3 * head_count)
    load(code_hbm, code_ref, 4 + 3 * head_count)
    for h in range(head_count):
        columns = pl.ds(h * width, width)
        load(q_hbm.at[:, columns], q_vm.at[0, h], 2 + 3 * h)
        load(do_hbm.at[:, columns], do_vm.at[0, h], 3 + 3 * h)
        load(o_hbm.at[:, columns], o_vm.at[h], 4 + 3 * h)
    for copy in loads[:2]:
        copy.wait()

    pl.semaphore_wait(barrier, 5)

    def remote(src, dst, send_sem, recv_sem, device):
        return pltpu.make_async_remote_copy(
            src_ref=src, dst_ref=dst, send_sem=send_sem, recv_sem=recv_sem,
            device_id=device, device_id_type=MESH)

    def kv_copy(slot, device):
        return remote(kv.at[0], kv.at[slot], kv_send.at[slot - 1], kv_recv.at[slot - 1], device)

    def wait_kv(slot):
        kv_copy(slot, mate).wait_recv()

    def pair_copy(src, dst, slot):
        return remote(src, dst, pair_send.at[slot], pair_recv.at[slot], mate)

    kv_sends = (kv_copy(pick(4, 5), later(4, 5)), kv_copy(pick(5, 3), later(5, 3)), kv_copy(6, later(6)), kv_copy(2, later(2)))
    for copy in kv_sends:
        copy.start()
    for copy in loads[2:]:
        copy.wait()
    pairs = (pair_copy(q_vm.at[0], q_vm.at[1], 0), pair_copy(do_vm.at[0], do_vm.at[1], 1),
             pair_copy(meta.at[0], meta.at[1], 2))
    dq_pair = pair_copy(dq_out, dq_in, 3)
    pairs[0].start()
    pairs[1].start()
    meta[0, pl.ds(0, head_count), :] = lse_ref[...]
    for h in range(head_count):
        product = do_vm[0, h].astype(jnp.float32) * o_vm[h].astype(jnp.float32)
        meta[0, pl.ds(head_count + h, 1), :] = jnp.sum(product.T, axis=0, keepdims=True)
    for at in range(steps - 1):
        meta[0, pl.ds(first_code + at, 1), :] = jnp.full((1, rows), code_ref[0, at].astype(jnp.float32))
    pairs[2].start()

    def g_copy(source, slot, device):
        return remote(g_out.at[source - 1], g_in.at[slot - 1], g_send.at[source - 1], g_recv.at[slot - 1], device)

    def position(device, shape, dim):
        u, w = device
        block = u * outer_count + w
        first, second = span_ref[2 * block], span_ref[2 * block + 1]
        at = lax.broadcasted_iota(jnp.int32, shape, dim)
        return jnp.where(at < half, first * half + at, second * half + at - half)

    features = head_count * rows

    def dot(x, y, dims):
        return lax.dot_general(x, y, (dims, ((), ())), preferred_element_type=jnp.float32)

    def reach(own, code_step):
        query_pos = position((inner_at, outer_at) if own == 0 else mate, (1, rows), 1)
        if code_step == 0:
            return query_pos
        row = first_code - 1 + (pick(5, 3) if code_step is None else code_step)
        code = meta[own, pl.ds(row, 1), :]
        limit = jnp.where(code == 2.0, jnp.int32(2 ** 31 - 1), jnp.int32(-1))
        return jnp.where(code == 1.0, query_pos, limit)

    def visit(slot, key_device, queries):
        key_block, value_block = kv[slot, 0], kv[slot, 1]
        first, count = queries[0][0], len(queries)
        q_all = q_vm[pl.ds(first, count)].reshape(count * features, width)
        do_all = do_vm[pl.ds(first, count)].reshape(count * features, width)
        key_pos = position(key_device, (rows, rows), 0)
        allowed, lse_rows, delta_rows = [], [], []
        for own, code_step in queries:
            allowed += [key_pos <= reach(own, code_step)] * head_count
            lse_rows += [meta[own, pl.ds(h, 1), :] for h in range(head_count)]
            delta_rows += [meta[own, pl.ds(head_count + h, 1), :] for h in range(head_count)]
        allowed, lse_row, delta_row = (jnp.concatenate(x, axis=1) for x in (allowed, lse_rows, delta_rows))
        scores = dot(key_block, q_all, ((1,), (1,))) * scale
        probs = jnp.where(allowed, jnp.exp(scores - lse_row), 0.0)
        dprob = dot(value_block, do_all, ((1,), (1,)))
        dscore = (probs * (dprob - delta_row) * scale).astype(jnp.bfloat16)
        value_part = dot(probs.astype(jnp.bfloat16), do_all, ((1,), (0,)))
        key_part = dot(dscore, q_all, ((1,), (0,)))
        query_part = dot(key_block.T, dscore, ((1,), (0,)))
        for at, (own, _) in enumerate(queries):
            dq_acc[own] += query_part[:, at * features:(at + 1) * features]
        return key_part, value_part

    def send_g(slot, device, parts):
        for part in range(2):
            g_out[slot - 1, part] = parts[part].astype(jnp.bfloat16)
        copy = g_copy(slot, slot, device)
        copy.start()
        return copy

    dq_acc[...] = jnp.zeros_like(dq_acc)
    own_acc[0], own_acc[1] = visit(0, (inner_at, outer_at), ((0, 0),))
    wait_kv(2)
    parts = visit(2, earlier(2), ((0, 2),))

    @pl.when(is_even)
    def _():
        send_g(2, earlier(2), parts)

    @pl.when(is_odd)
    def _():
        for part in range(2):
            held[part] = parts[part]

    for copy in pairs:
        copy.wait_recv()
    other = visit(pick(0, 2), shifted(pick(0, -2 % inner_count), 0), ((1, 1),))

    def send_dq():
        dq_out[...] = dq_acc[1].astype(jnp.bfloat16)
        dq_pair.start()

    @pl.when(is_even)
    def _():
        for part in range(2):
            own_acc[part] += other[part]
        send_dq()

    @pl.when(is_odd)
    def _():
        send_g(2, earlier(2), [held[part] + other[part] for part in range(2)])
        wait_kv(5)
        send_g(5, earlier(5), visit(5, earlier(5), ((0, 5), (1, 4))))
        wait_kv(4)
        send_g(4, earlier(4), visit(4, earlier(4), ((0, 4), (1, 3))))
        send_dq()

    wait_kv(pick(5, 3))
    send_g(pick(5, 3), earlier(5, 3), visit(pick(5, 3), earlier(5, 3), ((0, None),)))
    wait_kv(6)
    send_g(6, earlier(6), visit(6, earlier(6), ((0, 6),)))

    dq_pair.wait_recv()
    for h in range(head_count):
        columns = pl.ds(h * rows, rows)
        total = dq_acc[0, :, columns] + dq_in[:, columns].astype(jnp.float32)
        dq_ref[:, pl.ds(h * width, width)] = total.T.astype(jnp.bfloat16)

    last = (2, 6, 5, pick(4, 3))
    for slot in last:
        g_copy(slot, slot, mate).wait_recv()
    for part, out in ((0, dk_ref), (1, dv_ref)):
        total = own_acc[part]
        for slot in last:
            total = total + g_in[slot - 1, part].astype(jnp.float32)
        out[...] = total.astype(jnp.bfloat16)

    for copy in kv_sends + pairs + (dq_pair,):
        copy.wait_send()
    for slot in (2, pick(5, 3), 6):
        g_copy(slot, slot, mate).wait_send()

    @pl.when(is_odd)
    def _():
        for slot in (4, 5):
            g_copy(slot, slot, mate).wait_send()


def finish(dq_in, dk_in, dv_in, dq_out, dk_out, dv_out, sems):
    moves = [pltpu.make_async_copy(src, dst, sems.at[slot])
             for slot, (src, dst) in enumerate(((dq_in, dq_out), (dk_in, dk_out), (dv_in, dv_out)))]
    for move in moves:
        move.start()
    for move in moves:
        move.wait()


def shards(queries, keys, values, out_grad, forward_out, log_sum_exp, span_table, mask_codes):
    rows, features = queries.shape
    width = keys.shape[1]
    heads = log_sum_exp.shape[0]
    remote = len(WINDOW_PATH) - 1
    hbm = pl.BlockSpec(memory_space=pl.ANY)
    vmem = pl.BlockSpec(memory_space=pltpu.VMEM)
    grads = (
        jax.ShapeDtypeStruct((rows, features), jnp.bfloat16),
        jax.ShapeDtypeStruct((rows, width), jnp.bfloat16),
        jax.ShapeDtypeStruct((rows, width), jnp.bfloat16),
    )
    parts = pl.pallas_call(
        functools.partial(kernel, lax.axis_size("inner"), lax.axis_size("outer")),
        out_shape=grads,
        in_specs=[hbm] * 8,
        out_specs=(vmem, vmem, vmem),
        scratch_shapes=[
            pltpu.VMEM((heads, rows), jnp.float32),
            pltpu.SMEM(span_table.shape, jnp.int32),
            pltpu.SMEM(mask_codes.shape, jnp.int32),
            pltpu.VMEM((2, heads, rows, width), jnp.bfloat16),
            pltpu.VMEM((2, heads, rows, width), jnp.bfloat16),
            pltpu.VMEM((heads, rows, width), jnp.bfloat16),
            pltpu.VMEM((2, 2 * heads + 8, rows), jnp.float32),
            pltpu.VMEM((1 + remote, 2, rows, width), jnp.bfloat16),
            pltpu.VMEM((remote, 2, rows, width), jnp.bfloat16),
            pltpu.VMEM((remote, 2, rows, width), jnp.bfloat16),
            pltpu.VMEM((2, rows, width), jnp.float32),
            pltpu.VMEM((2, width, heads * rows), jnp.float32),
            pltpu.VMEM((width, heads * rows), jnp.bfloat16),
            pltpu.VMEM((width, heads * rows), jnp.bfloat16),
            pltpu.VMEM((2, rows, width), jnp.float32),
            pltpu.SemaphoreType.DMA((5 + 3 * heads,)),
            pltpu.SemaphoreType.DMA((remote,)),
            pltpu.SemaphoreType.DMA((remote,)),
            pltpu.SemaphoreType.DMA((remote,)),
            pltpu.SemaphoreType.DMA((remote,)),
            pltpu.SemaphoreType.DMA((4,)),
            pltpu.SemaphoreType.DMA((4,)),
        ],
        compiler_params=pltpu.CompilerParams(
            collective_id=0, has_side_effects=True, vmem_limit_bytes=16 * 2 ** 20),
    )(*(pltpu.with_memory_space_constraint(x, pltpu.HBM) for x in (queries, keys, values, out_grad, forward_out, log_sum_exp, span_table, mask_codes)))
    return pl.pallas_call(
        finish,
        out_shape=grads,
        in_specs=[hbm] * 3,
        out_specs=(hbm, hbm, hbm),
        scratch_shapes=[pltpu.SemaphoreType.DMA((3,))],
        compiler_params=pltpu.CompilerParams(vmem_limit_bytes=2 ** 20),
    )(*parts)


def solution(mesh):
    return jax.shard_map(
        shards,
        mesh=mesh,
        in_specs=(
            P(("inner", "outer"), None),
            P(("inner", "outer"), None),
            P(("inner", "outer"), None),
            P(("inner", "outer"), None),
            P(("inner", "outer"), None),
            P(None, ("inner", "outer")),
            P(),
            P(("inner", "outer"), None),
        ),
        out_specs=(
            P(("inner", "outer"), None),
            P(("inner", "outer"), None),
            P(("inner", "outer"), None),
        ),
        check_vma=False,
    )
```

```python
import functools

import jax
import jax.numpy as jnp
from jax import lax
from jax.experimental import pallas as pl
from jax.experimental.pallas import tpu as pltpu
from jax.sharding import PartitionSpec as P

WINDOW_PATH = ((0, 0), (1, 0), (2, 0), (2, 1), (3, 1), (4, 1), (4, 2))
MESH = pl.DeviceIdType.MESH


def kernel(inner_count, outer_count, q_hbm, k_hbm, v_hbm, do_hbm, o_hbm, lse_hbm, span_hbm, code_hbm,
           dq_ref, dk_ref, dv_ref,
           lse_ref, span_ref, code_ref, q_vm, do_vm, o_vm, meta, kv, g_out, g_in, held, dq_acc, dq_out, dq_in, own_acc,
           load_sem, kv_send, kv_recv, g_send, g_recv, pair_send, pair_recv):
    inner_at = lax.axis_index("inner")
    outer_at = lax.axis_index("outer")
    odd = lax.rem(inner_at, 2)
    is_even, is_odd = odd == 0, odd == 1
    outer_odd = lax.rem(outer_at, 2)
    _, head_count, rows, width = q_vm.shape
    half = rows // 2
    scale = width ** (-0.5)
    steps = len(WINDOW_PATH)
    first_code = 2 * head_count

    def pick(even, other):
        return even if even == other else even + odd * (other - even)

    def shifted(a, c):
        return lax.rem(inner_at + a, inner_count), lax.rem(outer_at + c, outer_count)

    def later(step, other=None):
        a, c = WINDOW_PATH[step]
        d, e = WINDOW_PATH[step if other is None else other]
        return shifted(pick(a % inner_count, d % inner_count), pick(c % outer_count, e % outer_count))

    def earlier(step, other=None):
        a, c = WINDOW_PATH[step]
        d, e = WINDOW_PATH[step if other is None else other]
        return shifted(pick(-a % inner_count, -d % inner_count), pick(-c % outer_count, -e % outer_count))

    mate = (inner_at + 1 - 2 * odd, outer_at)

    barrier = pltpu.get_barrier_semaphore()

    def greet(device):
        pl.semaphore_signal(barrier, inc=1, device_id=device, device_id_type=MESH)

    for step in (5, 6, 2):
        greet(earlier(step))

    @pl.when(is_odd)
    def _():
        greet(earlier(4))
        greet(earlier(3))

    greet(mate)
    loads = []

    def load(src, dst, slot):
        copy = pltpu.make_async_copy(src, dst, load_sem.at[slot])
        copy.start()
        loads.append(copy)

    load(k_hbm, kv.at[0, 0], 0)
    load(v_hbm, kv.at[0, 1], 1)
    load(lse_hbm, lse_ref, 2 + 3 * head_count)
    load(span_hbm, span_ref, 3 + 3 * head_count)
    load(code_hbm, code_ref, 4 + 3 * head_count)
    for h in range(head_count):
        columns = pl.ds(h * width, width)
        load(q_hbm.at[:, columns], q_vm.at[0, h], 2 + 3 * h)
        load(do_hbm.at[:, columns], do_vm.at[0, h], 3 + 3 * h)
        load(o_hbm.at[:, columns], o_vm.at[h], 4 + 3 * h)
    for copy in loads[:2]:
        copy.wait()

    pl.semaphore_wait(barrier, 5)

    def remote(src, dst, send_sem, recv_sem, device):
        return pltpu.make_async_remote_copy(
            src_ref=src, dst_ref=dst, send_sem=send_sem, recv_sem=recv_sem,
            device_id=device, device_id_type=MESH)

    def kv_copy(slot, device):
        return remote(kv.at[0], kv.at[slot], kv_send.at[slot - 1], kv_recv.at[slot - 1], device)

    def wait_kv(slot):
        kv_copy(slot, mate).wait_recv()

    def pair_copy(src, dst, slot):
        return remote(src, dst, pair_send.at[slot], pair_recv.at[slot], mate)

    kv_sends = (kv_copy(2, later(2)), kv_copy(6, later(6)), kv_copy(pick(4, 5), later(4, 5)), kv_copy(pick(5, 3), later(5, 3)))
    kv_sends[0].start()

    @pl.when(outer_odd == 0)
    def _():
        kv_sends[1].start()

    kv_sends[2].start()
    kv_sends[3].start()

    @pl.when(outer_odd == 1)
    def _():
        kv_sends[1].start()

    for copy in loads[2:]:
        copy.wait()
    pairs = (pair_copy(q_vm.at[0], q_vm.at[1], 0), pair_copy(do_vm.at[0], do_vm.at[1], 1),
             pair_copy(meta.at[0], meta.at[1], 2))
    dq_pair = pair_copy(dq_out, dq_in, 3)
    pairs[0].start()
    pairs[1].start()
    meta[0, pl.ds(0, head_count), :] = lse_ref[...]
    for h in range(head_count):
        product = do_vm[0, h].astype(jnp.float32) * o_vm[h].astype(jnp.float32)
        meta[0, pl.ds(head_count + h, 1), :] = jnp.sum(product.T, axis=0, keepdims=True)
    for at in range(steps - 1):
        meta[0, pl.ds(first_code + at, 1), :] = jnp.full((1, rows), code_ref[0, at].astype(jnp.float32))
    pairs[2].start()

    def g_copy(source, slot, device):
        return remote(g_out.at[source - 1], g_in.at[slot - 1], g_send.at[source - 1], g_recv.at[slot - 1], device)

    def position(device, shape, dim):
        u, w = device
        block = u * outer_count + w
        first, second = span_ref[2 * block], span_ref[2 * block + 1]
        at = lax.broadcasted_iota(jnp.int32, shape, dim)
        return jnp.where(at < half, first * half + at, second * half + at - half)

    features = head_count * rows

    def dot(x, y, dims):
        return lax.dot_general(x, y, (dims, ((), ())), preferred_element_type=jnp.float32)

    def reach(own, code_step):
        query_pos = position((inner_at, outer_at) if own == 0 else mate, (1, rows), 1)
        if code_step == 0:
            return query_pos
        row = first_code - 1 + (pick(5, 3) if code_step is None else code_step)
        code = meta[own, pl.ds(row, 1), :]
        limit = jnp.where(code == 2.0, jnp.int32(2 ** 31 - 1), jnp.int32(-1))
        return jnp.where(code == 1.0, query_pos, limit)

    def visit(slot, key_device, queries):
        key_block, value_block = kv[slot, 0], kv[slot, 1]
        first, count = queries[0][0], len(queries)
        q_all = q_vm[pl.ds(first, count)].reshape(count * features, width)
        do_all = do_vm[pl.ds(first, count)].reshape(count * features, width)
        key_pos = position(key_device, (rows, rows), 0)
        allowed, lse_rows, delta_rows = [], [], []
        for own, code_step in queries:
            allowed += [key_pos <= reach(own, code_step)] * head_count
            lse_rows += [meta[own, pl.ds(h, 1), :] for h in range(head_count)]
            delta_rows += [meta[own, pl.ds(head_count + h, 1), :] for h in range(head_count)]
        allowed, lse_row, delta_row = (jnp.concatenate(x, axis=1) for x in (allowed, lse_rows, delta_rows))
        scores = dot(key_block, q_all, ((1,), (1,))) * scale
        probs = jnp.where(allowed, jnp.exp(scores - lse_row), 0.0)
        dprob = dot(value_block, do_all, ((1,), (1,)))
        dscore = (probs * (dprob - delta_row) * scale).astype(jnp.bfloat16)
        value_part = dot(probs.astype(jnp.bfloat16), do_all, ((1,), (0,)))
        key_part = dot(dscore, q_all, ((1,), (0,)))
        query_part = dot(key_block.T, dscore, ((1,), (0,)))
        for at, (own, _) in enumerate(queries):
            dq_acc[own] += query_part[:, at * features:(at + 1) * features]
        return key_part, value_part

    def send_g(slot, device, parts):
        for part in range(2):
            g_out[slot - 1, part] = parts[part].astype(jnp.bfloat16)
        copy = g_copy(slot, slot, device)
        copy.start()
        return copy

    dq_acc[...] = jnp.zeros_like(dq_acc)
    own_acc[0], own_acc[1] = visit(0, (inner_at, outer_at), ((0, 0),))
    wait_kv(2)
    parts = visit(2, earlier(2), ((0, 2),))

    @pl.when(is_even)
    def _():
        send_g(2, earlier(2), parts)

    @pl.when(is_odd)
    def _():
        for part in range(2):
            held[part] = parts[part]

    for copy in pairs:
        copy.wait_recv()
    other = visit(pick(0, 2), shifted(pick(0, -2 % inner_count), 0), ((1, 1),))

    def send_dq():
        dq_out[...] = dq_acc[1].astype(jnp.bfloat16)
        dq_pair.start()

    @pl.when(is_even)
    def _():
        for part in range(2):
            own_acc[part] += other[part]
        send_dq()

    @pl.when(is_odd)
    def _():
        send_g(2, earlier(2), [held[part] + other[part] for part in range(2)])

    def last_step():
        wait_kv(6)
        send_g(6, earlier(6), visit(6, earlier(6), ((0, 6),)))

    pl.when(outer_odd == 0)(last_step)

    @pl.when(is_odd)
    def _():
        wait_kv(5)
        send_g(5, earlier(5), visit(5, earlier(5), ((0, 5), (1, 4))))
        wait_kv(4)
        send_g(4, earlier(4), visit(4, earlier(4), ((0, 4), (1, 3))))
        send_dq()

    wait_kv(pick(5, 3))
    send_g(pick(5, 3), earlier(5, 3), visit(pick(5, 3), earlier(5, 3), ((0, None),)))
    pl.when(outer_odd == 1)(last_step)

    dq_pair.wait_recv()
    for h in range(head_count):
        columns = pl.ds(h * rows, rows)
        total = dq_acc[0, :, columns] + dq_in[:, columns].astype(jnp.float32)
        dq_ref[:, pl.ds(h * width, width)] = total.T.astype(jnp.bfloat16)

    last = (2, 6, 5, pick(4, 3))
    for slot in last:
        g_copy(slot, slot, mate).wait_recv()
    for part, out in ((0, dk_ref), (1, dv_ref)):
        total = own_acc[part]
        for slot in last:
            total = total + g_in[slot - 1, part].astype(jnp.float32)
        out[...] = total.astype(jnp.bfloat16)

    for copy in kv_sends + pairs + (dq_pair,):
        copy.wait_send()
    for slot in (2, pick(5, 3), 6):
        g_copy(slot, slot, mate).wait_send()

    @pl.when(is_odd)
    def _():
        for slot in (4, 5):
            g_copy(slot, slot, mate).wait_send()


def finish(dq_in, dk_in, dv_in, dq_out, dk_out, dv_out, sems):
    moves = [pltpu.make_async_copy(src, dst, sems.at[slot])
             for slot, (src, dst) in enumerate(((dq_in, dq_out), (dk_in, dk_out), (dv_in, dv_out)))]
    for move in moves:
        move.start()
    for move in moves:
        move.wait()


def shards(queries, keys, values, out_grad, forward_out, log_sum_exp, span_table, mask_codes):
    rows, features = queries.shape
    width = keys.shape[1]
    heads = log_sum_exp.shape[0]
    remote = len(WINDOW_PATH) - 1
    hbm = pl.BlockSpec(memory_space=pl.ANY)
    vmem = pl.BlockSpec(memory_space=pltpu.VMEM)
    grads = (
        jax.ShapeDtypeStruct((rows, features), jnp.bfloat16),
        jax.ShapeDtypeStruct((rows, width), jnp.bfloat16),
        jax.ShapeDtypeStruct((rows, width), jnp.bfloat16),
    )
    parts = pl.pallas_call(
        functools.partial(kernel, lax.axis_size("inner"), lax.axis_size("outer")),
        out_shape=grads,
        in_specs=[hbm] * 8,
        out_specs=(vmem, vmem, vmem),
        scratch_shapes=[
            pltpu.VMEM((heads, rows), jnp.float32),
            pltpu.SMEM(span_table.shape, jnp.int32),
            pltpu.SMEM(mask_codes.shape, jnp.int32),
            pltpu.VMEM((2, heads, rows, width), jnp.bfloat16),
            pltpu.VMEM((2, heads, rows, width), jnp.bfloat16),
            pltpu.VMEM((heads, rows, width), jnp.bfloat16),
            pltpu.VMEM((2, 2 * heads + 8, rows), jnp.float32),
            pltpu.VMEM((1 + remote, 2, rows, width), jnp.bfloat16),
            pltpu.VMEM((remote, 2, rows, width), jnp.bfloat16),
            pltpu.VMEM((remote, 2, rows, width), jnp.bfloat16),
            pltpu.VMEM((2, rows, width), jnp.float32),
            pltpu.VMEM((2, width, heads * rows), jnp.float32),
            pltpu.VMEM((width, heads * rows), jnp.bfloat16),
            pltpu.VMEM((width, heads * rows), jnp.bfloat16),
            pltpu.VMEM((2, rows, width), jnp.float32),
            pltpu.SemaphoreType.DMA((5 + 3 * heads,)),
            pltpu.SemaphoreType.DMA((remote,)),
            pltpu.SemaphoreType.DMA((remote,)),
            pltpu.SemaphoreType.DMA((remote,)),
            pltpu.SemaphoreType.DMA((remote,)),
            pltpu.SemaphoreType.DMA((4,)),
            pltpu.SemaphoreType.DMA((4,)),
        ],
        compiler_params=pltpu.CompilerParams(
            collective_id=0, has_side_effects=True, vmem_limit_bytes=16 * 2 ** 20),
    )(*(pltpu.with_memory_space_constraint(x, pltpu.HBM) for x in (queries, keys, values, out_grad, forward_out, log_sum_exp, span_table, mask_codes)))
    return pl.pallas_call(
        finish,
        out_shape=grads,
        in_specs=[hbm] * 3,
        out_specs=(hbm, hbm, hbm),
        scratch_shapes=[pltpu.SemaphoreType.DMA((3,))],
        compiler_params=pltpu.CompilerParams(vmem_limit_bytes=2 ** 20),
    )(*parts)


def solution(mesh):
    return jax.shard_map(
        shards,
        mesh=mesh,
        in_specs=(
            P(("inner", "outer"), None),
            P(("inner", "outer"), None),
            P(("inner", "outer"), None),
            P(("inner", "outer"), None),
            P(("inner", "outer"), None),
            P(None, ("inner", "outer")),
            P(),
            P(("inner", "outer"), None),
        ),
        out_specs=(
            P(("inner", "outer"), None),
            P(("inner", "outer"), None),
            P(("inner", "outer"), None),
        ),
        check_vma=False,
    )
```

```python
import functools
import math

import jax
import jax.numpy as jnp
from jax import lax
from jax.experimental import pallas as pl
from jax.experimental.pallas import tpu as pltpu
from jax.sharding import PartitionSpec as P

WINDOW_PATH = ((0, 0), (1, 0), (2, 0), (2, 1), (3, 1), (4, 1), (4, 2))
MESH = pl.DeviceIdType.MESH
LOG2_E = math.log2(math.e)


def kernel(inner_count, outer_count, q_hbm, k_hbm, v_hbm, do_hbm, o_hbm, lse_hbm, span_hbm, code_hbm,
           dq_ref, dk_ref, dv_ref,
           lse_ref, span_ref, code_ref, q_vm, do_vm, o_vm, meta, kv, g_out, g_in, dq_acc, dq_out, dq_in, own_acc,
           load_sem, kv_send, kv_recv, g_send, g_recv, pair_send, pair_recv):
    inner_at = lax.axis_index("inner")
    outer_at = lax.axis_index("outer")
    odd = lax.rem(inner_at, 2)
    is_even, is_odd = odd == 0, odd == 1
    outer_odd = lax.rem(outer_at, 2)
    _, head_count, rows, width = q_vm.shape
    half = rows // 2
    scale = width ** (-0.5)
    steps = len(WINDOW_PATH)
    first_code = 2 * head_count

    def pick(even, other):
        return even if even == other else even + odd * (other - even)

    def shifted(a, c):
        return lax.rem(inner_at + a, inner_count), lax.rem(outer_at + c, outer_count)

    def later(step, other=None):
        a, c = WINDOW_PATH[step]
        d, e = WINDOW_PATH[step if other is None else other]
        return shifted(pick(a % inner_count, d % inner_count), pick(c % outer_count, e % outer_count))

    def earlier(step, other=None):
        a, c = WINDOW_PATH[step]
        d, e = WINDOW_PATH[step if other is None else other]
        return shifted(pick(-a % inner_count, -d % inner_count), pick(-c % outer_count, -e % outer_count))

    mate = (inner_at + 1 - 2 * odd, outer_at)

    barrier = pltpu.get_barrier_semaphore()

    def greet(device):
        pl.semaphore_signal(barrier, inc=1, device_id=device, device_id_type=MESH)

    ahead = shifted(pick(-1 % inner_count, 2 % inner_count), 0)
    for device in (earlier(5), earlier(6), ahead, earlier(2, 4)):
        greet(device)
    greet(mate)
    loads = []

    def load(src, dst, slot):
        copy = pltpu.make_async_copy(src, dst, load_sem.at[slot])
        copy.start()
        loads.append(copy)

    load(k_hbm, kv.at[0, 0], 0)
    load(v_hbm, kv.at[0, 1], 1)
    load(lse_hbm, lse_ref, 2 + 3 * head_count)
    load(span_hbm, span_ref, 3 + 3 * head_count)
    load(code_hbm, code_ref, 4 + 3 * head_count)
    for h in range(head_count):
        columns = pl.ds(h * width, width)
        load(q_hbm.at[:, columns], q_vm.at[0, h], 2 + 3 * h)
        load(do_hbm.at[:, columns], do_vm.at[0, h], 3 + 3 * h)
        load(o_hbm.at[:, columns], o_vm.at[h], 4 + 3 * h)
    for copy in loads[:2]:
        copy.wait()

    pl.semaphore_wait(barrier, 5)

    def remote(src, dst, send_sem, recv_sem, device):
        return pltpu.make_async_remote_copy(
            src_ref=src, dst_ref=dst, send_sem=send_sem, recv_sem=recv_sem,
            device_id=device, device_id_type=MESH)

    def kv_copy(slot, device):
        return remote(kv.at[0], kv.at[slot], kv_send.at[slot - 1], kv_recv.at[slot - 1], device)

    def wait_kv(slot):
        kv_copy(slot, mate).wait_recv()

    def pair_copy(src, dst, slot):
        return remote(src, dst, pair_send.at[slot], pair_recv.at[slot], mate)

    kv_sends = (kv_copy(pick(2, 1), later(2, 1)), kv_copy(6, later(6)), kv_copy(pick(4, 5), later(4, 5)))
    kv_even = kv_copy(5, later(5))
    relay = remote(kv.at[5], kv.at[3], kv_send.at[2], kv_recv.at[2], earlier(2))
    kv_sends[0].start()

    @pl.when(outer_odd == 0)
    def _():
        kv_sends[1].start()

    kv_sends[2].start()
    pl.when(is_even)(kv_even.start)

    @pl.when(outer_odd == 1)
    def _():
        kv_sends[1].start()

    for copy in loads[2:]:
        copy.wait()
    pairs = (pair_copy(q_vm.at[0], q_vm.at[1], 0), pair_copy(do_vm.at[0], do_vm.at[1], 1),
             pair_copy(meta.at[0], meta.at[1], 2))
    dq_pair = pair_copy(dq_out, dq_in, 3)
    pairs[0].start()
    pairs[1].start()
    meta[0, pl.ds(0, head_count), :] = lse_ref[...] * LOG2_E
    for h in range(head_count):
        product = do_vm[0, h].astype(jnp.float32) * o_vm[h].astype(jnp.float32)
        meta[0, pl.ds(head_count + h, 1), :] = jnp.sum(product.T, axis=0, keepdims=True)
    for at in range(steps - 1):
        meta[0, pl.ds(first_code + at, 1), :] = jnp.full((1, rows), code_ref[0, at].astype(jnp.float32))
    pairs[2].start()

    def g_copy(source, slot, device):
        return remote(g_out.at[source - 1], g_in.at[slot - 1], g_send.at[source - 1], g_recv.at[slot - 1], device)

    def position(device, shape, dim):
        u, w = device
        block = u * outer_count + w
        first, second = span_ref[2 * block], span_ref[2 * block + 1]
        at = lax.broadcasted_iota(jnp.int32, shape, dim)
        return jnp.where(at < half, first * half + at, second * half + at - half)

    features = head_count * rows

    def dot(x, y, dims):
        return lax.dot_general(x, y, (dims, ((), ())), preferred_element_type=jnp.float32)

    def reach(own, code_step):
        query_pos = position((inner_at, outer_at) if own == 0 else mate, (1, rows), 1)
        if code_step == 0:
            return query_pos
        row = first_code - 1 + (pick(5, 3) if code_step is None else code_step)
        code = meta[own, pl.ds(row, 1), :]
        limit = jnp.where(code == 2.0, jnp.int32(2 ** 31 - 1), jnp.int32(-1))
        return jnp.where(code == 1.0, query_pos, limit)

    def visit(slot, key_device, queries):
        key_block, value_block = kv[slot, 0], kv[slot, 1]
        first, count = queries[0][0], len(queries)
        q_all = q_vm[pl.ds(first, count)].reshape(count * features, width)
        do_all = do_vm[pl.ds(first, count)].reshape(count * features, width)
        key_pos = position(key_device, (rows, rows), 0)
        allowed, lse_rows, delta_rows = [], [], []
        for own, code_step in queries:
            allowed += [key_pos <= reach(own, code_step)] * head_count
            lse_rows += [meta[own, pl.ds(h, 1), :] for h in range(head_count)]
            delta_rows += [meta[own, pl.ds(head_count + h, 1), :] for h in range(head_count)]
        allowed, lse_row, delta_row = (jnp.concatenate(x, axis=1) for x in (allowed, lse_rows, delta_rows))
        scores = dot(key_block, q_all, ((1,), (1,))) * (scale * LOG2_E)
        probs = jnp.where(allowed, jnp.exp2(scores - lse_row), 0.0)
        dprob = dot(value_block, do_all, ((1,), (1,)))
        dscore = (probs * (dprob - delta_row)).astype(jnp.bfloat16)
        value_part = dot(probs.astype(jnp.bfloat16), do_all, ((1,), (0,)))
        key_part = dot(dscore, q_all, ((1,), (0,)))
        query_part = dot(key_block.T, dscore, ((1,), (0,)))
        for at, (own, _) in enumerate(queries):
            dq_acc[own] += query_part[:, at * features:(at + 1) * features]
        return key_part, value_part

    def send_g(slot, device, parts):
        g_out[slot - 1, 0] = (parts[0] * scale).astype(jnp.bfloat16)
        g_out[slot - 1, 1] = parts[1].astype(jnp.bfloat16)
        copy = g_copy(slot, slot, device)
        copy.start()
        return copy

    dq_acc[...] = jnp.zeros_like(dq_acc)
    own_acc[0], own_acc[1] = visit(0, (inner_at, outer_at), ((0, 0),))
    for copy in pairs:
        copy.wait_recv()
    def send_dq():
        dq_out[...] = (dq_acc[1] * scale).astype(jnp.bfloat16)
        dq_pair.start()

    @pl.when(is_even)
    def _():
        other = visit(0, (inner_at, outer_at), ((1, 1),))
        for part in range(2):
            own_acc[part] += other[part]
        wait_kv(1)
        send_g(1, earlier(1), visit(1, earlier(1), ((0, 1), (1, 2))))
        send_dq()
        wait_kv(2)
        send_g(2, earlier(2), visit(2, earlier(2), ((0, 2),)))

    def last_step():
        wait_kv(6)
        send_g(6, earlier(6), visit(6, earlier(6), ((0, 6),)))

    pl.when(outer_odd == 0)(last_step)

    @pl.when(is_odd)
    def _():
        wait_kv(5)
        relay.start()
        send_g(5, earlier(5), visit(5, earlier(5), ((0, 5), (1, 4))))
        wait_kv(4)
        send_g(4, earlier(4), visit(4, earlier(4), ((0, 4), (1, 3))))
        send_dq()

    wait_kv(pick(5, 3))
    send_g(pick(5, 3), earlier(5, 3), visit(pick(5, 3), earlier(5, 3), ((0, None),)))
    pl.when(outer_odd == 1)(last_step)

    dq_pair.wait_recv()
    for h in range(head_count):
        columns = pl.ds(h * rows, rows)
        total = dq_acc[0, :, columns] * scale + dq_in[:, columns].astype(jnp.float32)
        dq_ref[:, pl.ds(h * width, width)] = total.T.astype(jnp.bfloat16)

    last = (pick(2, 1), 6, 5, pick(4, 3))
    own_acc[0] *= scale
    for slot in last[:-1]:
        g_copy(slot, slot, mate).wait_recv()
        own_acc[...] += g_in[slot - 1].astype(jnp.float32)
    g_copy(last[-1], last[-1], mate).wait_recv()
    for part, out in ((0, dk_ref), (1, dv_ref)):
        out[...] = (own_acc[part] + g_in[last[-1] - 1, part].astype(jnp.float32)).astype(jnp.bfloat16)

    for copy in kv_sends + pairs + (dq_pair,):
        copy.wait_send()
    pl.when(is_even)(kv_even.wait_send)
    pl.when(is_odd)(relay.wait_send)
    for slot in (pick(1, 4), pick(2, 3), 5, 6):
        g_copy(slot, slot, mate).wait_send()


def finish(dq_in, dk_in, dv_in, dq_out, dk_out, dv_out, sems):
    moves = [pltpu.make_async_copy(src, dst, sems.at[slot])
             for slot, (src, dst) in enumerate(((dq_in, dq_out), (dk_in, dk_out), (dv_in, dv_out)))]
    for move in moves:
        move.start()
    for move in moves:
        move.wait()


def shards(queries, keys, values, out_grad, forward_out, log_sum_exp, span_table, mask_codes):
    rows, features = queries.shape
    width = keys.shape[1]
    heads = log_sum_exp.shape[0]
    remote = len(WINDOW_PATH) - 1
    hbm = pl.BlockSpec(memory_space=pl.ANY)
    vmem = pl.BlockSpec(memory_space=pltpu.VMEM)
    grads = (
        jax.ShapeDtypeStruct((rows, features), jnp.bfloat16),
        jax.ShapeDtypeStruct((rows, width), jnp.bfloat16),
        jax.ShapeDtypeStruct((rows, width), jnp.bfloat16),
    )
    parts = pl.pallas_call(
        functools.partial(kernel, lax.axis_size("inner"), lax.axis_size("outer")),
        out_shape=grads,
        in_specs=[hbm] * 8,
        out_specs=(vmem, vmem, vmem),
        scratch_shapes=[
            pltpu.VMEM((heads, rows), jnp.float32),
            pltpu.SMEM(span_table.shape, jnp.int32),
            pltpu.SMEM(mask_codes.shape, jnp.int32),
            pltpu.VMEM((2, heads, rows, width), jnp.bfloat16),
            pltpu.VMEM((2, heads, rows, width), jnp.bfloat16),
            pltpu.VMEM((heads, rows, width), jnp.bfloat16),
            pltpu.VMEM((2, 2 * heads + 8, rows), jnp.float32),
            pltpu.VMEM((1 + remote, 2, rows, width), jnp.bfloat16),
            pltpu.VMEM((remote, 2, rows, width), jnp.bfloat16),
            pltpu.VMEM((remote, 2, rows, width), jnp.bfloat16),
            pltpu.VMEM((2, width, heads * rows), jnp.float32),
            pltpu.VMEM((width, heads * rows), jnp.bfloat16),
            pltpu.VMEM((width, heads * rows), jnp.bfloat16),
            pltpu.VMEM((2, rows, width), jnp.float32),
            pltpu.SemaphoreType.DMA((5 + 3 * heads,)),
            pltpu.SemaphoreType.DMA((remote,)),
            pltpu.SemaphoreType.DMA((remote,)),
            pltpu.SemaphoreType.DMA((remote,)),
            pltpu.SemaphoreType.DMA((remote,)),
            pltpu.SemaphoreType.DMA((4,)),
            pltpu.SemaphoreType.DMA((4,)),
        ],
        compiler_params=pltpu.CompilerParams(
            collective_id=0, has_side_effects=True, vmem_limit_bytes=16 * 2 ** 20),
    )(*(pltpu.with_memory_space_constraint(x, pltpu.HBM) for x in (queries, keys, values, out_grad, forward_out, log_sum_exp, span_table, mask_codes)))
    return pl.pallas_call(
        finish,
        out_shape=grads,
        in_specs=[hbm] * 3,
        out_specs=(hbm, hbm, hbm),
        scratch_shapes=[pltpu.SemaphoreType.DMA((3,))],
        compiler_params=pltpu.CompilerParams(vmem_limit_bytes=2 ** 20),
    )(*parts)


def solution(mesh):
    return jax.shard_map(
        shards,
        mesh=mesh,
        in_specs=(
            P(("inner", "outer"), None),
            P(("inner", "outer"), None),
            P(("inner", "outer"), None),
            P(("inner", "outer"), None),
            P(("inner", "outer"), None),
            P(None, ("inner", "outer")),
            P(),
            P(("inner", "outer"), None),
        ),
        out_specs=(
            P(("inner", "outer"), None),
            P(("inner", "outer"), None),
            P(("inner", "outer"), None),
        ),
        check_vma=False,
    )
```

```python
import functools
import math

import jax
import jax.numpy as jnp
from jax import lax
from jax.experimental import pallas as pl
from jax.experimental.pallas import tpu as pltpu
from jax.sharding import PartitionSpec as P

WINDOW_PATH = ((0, 0), (1, 0), (2, 0), (2, 1), (3, 1), (4, 1), (4, 2))
MESH = pl.DeviceIdType.MESH
LOG2_E = math.log2(math.e)


def kernel(inner_count, outer_count, q_hbm, k_hbm, v_hbm, do_hbm, o_hbm, lse_hbm, span_hbm, code_hbm,
           dq_ref, dk_ref, dv_ref,
           lse_ref, span_ref, code_ref, q_vm, do_vm, o_vm, meta, kv, g_out, g_in, dq_acc, dq_out, dq_in, own_acc,
           load_sem, kv_send, kv_recv, g_send, g_recv, pair_send, pair_recv):
    inner_at = lax.axis_index("inner")
    outer_at = lax.axis_index("outer")
    odd = lax.rem(inner_at, 2)
    is_even, is_odd = odd == 0, odd == 1
    outer_odd = lax.rem(outer_at, 2)
    _, head_count, rows, width = q_vm.shape
    half = rows // 2
    scale = width ** (-0.5)
    steps = len(WINDOW_PATH)
    first_code = 2 * head_count

    def pick(even, other):
        return even if even == other else even + odd * (other - even)

    def shifted(a, c):
        return lax.rem(inner_at + a, inner_count), lax.rem(outer_at + c, outer_count)

    def later(step, other=None):
        a, c = WINDOW_PATH[step]
        d, e = WINDOW_PATH[step if other is None else other]
        return shifted(pick(a % inner_count, d % inner_count), pick(c % outer_count, e % outer_count))

    def earlier(step, other=None):
        a, c = WINDOW_PATH[step]
        d, e = WINDOW_PATH[step if other is None else other]
        return shifted(pick(-a % inner_count, -d % inner_count), pick(-c % outer_count, -e % outer_count))

    mate = (inner_at + 1 - 2 * odd, outer_at)

    barrier = pltpu.get_barrier_semaphore()

    def greet(device):
        pl.semaphore_signal(barrier, inc=1, device_id=device, device_id_type=MESH)

    ahead = shifted(pick(-1 % inner_count, 2 % inner_count), 0)
    for device in (earlier(5), earlier(6), ahead, earlier(2, 4)):
        greet(device)
    greet(mate)
    loads = []

    def load(src, dst, slot):
        copy = pltpu.make_async_copy(src, dst, load_sem.at[slot])
        copy.start()
        loads.append(copy)

    load(k_hbm, kv.at[0, 0], 0)
    load(v_hbm, kv.at[0, 1], 1)
    load(lse_hbm, lse_ref, 2 + 3 * head_count)
    load(span_hbm, span_ref, 3 + 3 * head_count)
    load(code_hbm, code_ref, 4 + 3 * head_count)
    for h in range(head_count):
        columns = pl.ds(h * width, width)
        load(q_hbm.at[:, columns], q_vm.at[0, h], 2 + 3 * h)
        load(do_hbm.at[:, columns], do_vm.at[0, h], 3 + 3 * h)
        load(o_hbm.at[:, columns], o_vm.at[h], 4 + 3 * h)
    for copy in loads[:2]:
        copy.wait()

    pl.semaphore_wait(barrier, 5)

    def remote(src, dst, send_sem, recv_sem, device):
        return pltpu.make_async_remote_copy(
            src_ref=src, dst_ref=dst, send_sem=send_sem, recv_sem=recv_sem,
            device_id=device, device_id_type=MESH)

    def kv_copy(slot, device, source=0, to=None):
        to = slot if to is None else to
        return [remote(kv.at[source, part], kv.at[to, part], kv_send.at[slot - 1, part], kv_recv.at[to - 1, part], device)
                for part in range(2)]

    def wait_kv(slot, part):
        remote(kv.at[0, part], kv.at[slot, part], kv_send.at[slot - 1, part], kv_recv.at[slot - 1, part], mate).wait_recv()

    def begin(copies):
        for copy in copies:
            copy.start()

    def done(copies):
        for copy in copies:
            copy.wait_send()

    def pair_copy(src, dst, slot):
        return remote(src, dst, pair_send.at[slot], pair_recv.at[slot], mate)

    kv_sends = (kv_copy(pick(2, 1), later(2, 1)), kv_copy(6, later(6)), kv_copy(pick(4, 5), later(4, 5)))
    kv_even = kv_copy(5, later(5))
    relay = kv_copy(3, earlier(2), 5)
    begin(kv_sends[0])

    @pl.when(outer_odd == 0)
    def _():
        begin(kv_sends[1])

    begin(kv_sends[2])
    pl.when(is_even)(functools.partial(begin, kv_even))

    @pl.when(outer_odd == 1)
    def _():
        begin(kv_sends[1])

    for copy in loads[2:]:
        copy.wait()
    pairs = (pair_copy(q_vm.at[0], q_vm.at[1], 0), pair_copy(do_vm.at[0], do_vm.at[1], 1),
             pair_copy(meta.at[0], meta.at[1], 2))
    dq_pair = pair_copy(dq_out, dq_in, 3)
    pairs[0].start()
    pairs[1].start()
    meta[0, pl.ds(0, head_count), :] = lse_ref[...] * LOG2_E
    for h in range(head_count):
        product = do_vm[0, h].astype(jnp.float32) * o_vm[h].astype(jnp.float32)
        meta[0, pl.ds(head_count + h, 1), :] = jnp.sum(product.T, axis=0, keepdims=True)
    for at in range(steps - 1):
        meta[0, pl.ds(first_code + at, 1), :] = jnp.full((1, rows), code_ref[0, at].astype(jnp.float32))
    pairs[2].start()

    def g_copy(slot, part, device):
        return remote(g_out.at[slot - 1, part], g_in.at[slot - 1, part], g_send.at[slot - 1, part], g_recv.at[slot - 1, part], device)

    def position(device, shape, dim):
        u, w = device
        block = u * outer_count + w
        first, second = span_ref[2 * block], span_ref[2 * block + 1]
        at = lax.broadcasted_iota(jnp.int32, shape, dim)
        return jnp.where(at < half, first * half + at, second * half + at - half)

    features = head_count * rows

    def dot(x, y, dims):
        return lax.dot_general(x, y, (dims, ((), ())), preferred_element_type=jnp.float32)

    def reach(own, code_step):
        query_pos = position((inner_at, outer_at) if own == 0 else mate, (1, rows), 1)
        if code_step == 0:
            return query_pos
        row = first_code - 1 + (pick(5, 3) if code_step is None else code_step)
        code = meta[own, pl.ds(row, 1), :]
        limit = jnp.where(code == 2.0, jnp.int32(2 ** 31 - 1), jnp.int32(-1))
        return jnp.where(code == 1.0, query_pos, limit)

    def visit(slot, key_device, queries, arrive, give):
        arrive(0)
        key_block = kv[slot, 0]
        first, count = queries[0][0], len(queries)
        q_all = q_vm[pl.ds(first, count)].reshape(count * features, width)
        do_all = do_vm[pl.ds(first, count)].reshape(count * features, width)
        key_pos = position(key_device, (rows, rows), 0)
        allowed, lse_rows, delta_rows = [], [], []
        for own, code_step in queries:
            allowed += [key_pos <= reach(own, code_step)] * head_count
            lse_rows += [meta[own, pl.ds(h, 1), :] for h in range(head_count)]
            delta_rows += [meta[own, pl.ds(head_count + h, 1), :] for h in range(head_count)]
        allowed, lse_row, delta_row = (jnp.concatenate(x, axis=1) for x in (allowed, lse_rows, delta_rows))
        scores = dot(key_block, q_all, ((1,), (1,))) * (scale * LOG2_E)
        probs = jnp.where(allowed, jnp.exp2(scores - lse_row), 0.0)
        give(1, dot(probs.astype(jnp.bfloat16), do_all, ((1,), (0,))))
        arrive(1)
        dprob = dot(kv[slot, 1], do_all, ((1,), (1,)))
        dscore = (probs * (dprob - delta_row)).astype(jnp.bfloat16)
        give(0, dot(dscore, q_all, ((1,), (0,))))
        query_part = dot(key_block.T, dscore, ((1,), (0,)))
        for at, (own, _) in enumerate(queries):
            dq_acc[own] += query_part[:, at * features:(at + 1) * features]

    def send_g(slot, device):
        def give(part, value):
            g_out[slot - 1, part] = (value if part else value * scale).astype(jnp.bfloat16)
            g_copy(slot, part, device).start()

        return give

    def come(slot):
        return lambda part: wait_kv(slot, part)

    def keep(part, value):
        own_acc[part] = value

    def add(part, value):
        own_acc[part] += value

    def nothing(part):
        pass

    dq_acc[...] = jnp.zeros_like(dq_acc)
    visit(0, (inner_at, outer_at), ((0, 0),), nothing, keep)
    for copy in pairs:
        copy.wait_recv()
    def send_dq():
        dq_out[...] = (dq_acc[1] * scale).astype(jnp.bfloat16)
        dq_pair.start()

    @pl.when(is_even)
    def _():
        visit(0, (inner_at, outer_at), ((1, 1),), nothing, add)
        visit(1, earlier(1), ((0, 1), (1, 2)), come(1), send_g(1, earlier(1)))
        send_dq()
        visit(2, earlier(2), ((0, 2),), come(2), send_g(2, earlier(2)))

    def last_step():
        visit(6, earlier(6), ((0, 6),), come(6), send_g(6, earlier(6)))

    pl.when(outer_odd == 0)(last_step)

    def hand_on(part):
        wait_kv(5, part)
        relay[part].start()

    @pl.when(is_odd)
    def _():
        visit(5, earlier(5), ((0, 5), (1, 4)), hand_on, send_g(5, earlier(5)))
        visit(4, earlier(4), ((0, 4), (1, 3)), come(4), send_g(4, earlier(4)))

    near = pick(5, 3)
    visit(near, earlier(5, 3), ((0, None),), come(near), send_g(near, earlier(5, 3)))
    pl.when(is_odd)(send_dq)
    pl.when(outer_odd == 1)(last_step)

    dq_pair.wait_recv()
    for h in range(head_count):
        columns = pl.ds(h * rows, rows)
        total = dq_acc[0, :, columns] * scale + dq_in[:, columns].astype(jnp.float32)
        dq_ref[:, pl.ds(h * width, width)] = total.T.astype(jnp.bfloat16)

    last = (pick(2, 1), 6, 5, pick(4, 3))
    own_acc[0] *= scale
    for slot in last[:-1]:
        for part in (1, 0):
            g_copy(slot, part, mate).wait_recv()
        own_acc[...] += g_in[slot - 1].astype(jnp.float32)
    for part, out in ((1, dv_ref), (0, dk_ref)):
        g_copy(last[-1], part, mate).wait_recv()
        out[...] = (own_acc[part] + g_in[last[-1] - 1, part].astype(jnp.float32)).astype(jnp.bfloat16)

    for copy in pairs + (dq_pair,):
        copy.wait_send()
    for copies in kv_sends:
        done(copies)
    pl.when(is_even)(functools.partial(done, kv_even))
    pl.when(is_odd)(functools.partial(done, relay))
    for slot in (pick(1, 4), pick(2, 3), 5, 6):
        for part in range(2):
            g_copy(slot, part, mate).wait_send()


def finish(dq_in, dk_in, dv_in, dq_out, dk_out, dv_out, sems):
    moves = [pltpu.make_async_copy(src, dst, sems.at[slot])
             for slot, (src, dst) in enumerate(((dq_in, dq_out), (dk_in, dk_out), (dv_in, dv_out)))]
    for move in moves:
        move.start()
    for move in moves:
        move.wait()


def shards(queries, keys, values, out_grad, forward_out, log_sum_exp, span_table, mask_codes):
    rows, features = queries.shape
    width = keys.shape[1]
    heads = log_sum_exp.shape[0]
    remote = len(WINDOW_PATH) - 1
    hbm = pl.BlockSpec(memory_space=pl.ANY)
    vmem = pl.BlockSpec(memory_space=pltpu.VMEM)
    grads = (
        jax.ShapeDtypeStruct((rows, features), jnp.bfloat16),
        jax.ShapeDtypeStruct((rows, width), jnp.bfloat16),
        jax.ShapeDtypeStruct((rows, width), jnp.bfloat16),
    )
    parts = pl.pallas_call(
        functools.partial(kernel, lax.axis_size("inner"), lax.axis_size("outer")),
        out_shape=grads,
        in_specs=[hbm] * 8,
        out_specs=(vmem, vmem, vmem),
        scratch_shapes=[
            pltpu.VMEM((heads, rows), jnp.float32),
            pltpu.SMEM(span_table.shape, jnp.int32),
            pltpu.SMEM(mask_codes.shape, jnp.int32),
            pltpu.VMEM((2, heads, rows, width), jnp.bfloat16),
            pltpu.VMEM((2, heads, rows, width), jnp.bfloat16),
            pltpu.VMEM((heads, rows, width), jnp.bfloat16),
            pltpu.VMEM((2, 2 * heads + 8, rows), jnp.float32),
            pltpu.VMEM((1 + remote, 2, rows, width), jnp.bfloat16),
            pltpu.VMEM((remote, 2, rows, width), jnp.bfloat16),
            pltpu.VMEM((remote, 2, rows, width), jnp.bfloat16),
            pltpu.VMEM((2, width, heads * rows), jnp.float32),
            pltpu.VMEM((width, heads * rows), jnp.bfloat16),
            pltpu.VMEM((width, heads * rows), jnp.bfloat16),
            pltpu.VMEM((2, rows, width), jnp.float32),
            pltpu.SemaphoreType.DMA((5 + 3 * heads,)),
            pltpu.SemaphoreType.DMA((remote, 2)),
            pltpu.SemaphoreType.DMA((remote, 2)),
            pltpu.SemaphoreType.DMA((remote, 2)),
            pltpu.SemaphoreType.DMA((remote, 2)),
            pltpu.SemaphoreType.DMA((4,)),
            pltpu.SemaphoreType.DMA((4,)),
        ],
        compiler_params=pltpu.CompilerParams(
            collective_id=0, has_side_effects=True, vmem_limit_bytes=16 * 2 ** 20),
    )(*(pltpu.with_memory_space_constraint(x, pltpu.HBM) for x in (queries, keys, values, out_grad, forward_out, log_sum_exp, span_table, mask_codes)))
    return pl.pallas_call(
        finish,
        out_shape=grads,
        in_specs=[hbm] * 3,
        out_specs=(hbm, hbm, hbm),
        scratch_shapes=[pltpu.SemaphoreType.DMA((3,))],
        compiler_params=pltpu.CompilerParams(vmem_limit_bytes=2 ** 20),
    )(*parts)


def solution(mesh):
    return jax.shard_map(
        shards,
        mesh=mesh,
        in_specs=(
            P(("inner", "outer"), None),
            P(("inner", "outer"), None),
            P(("inner", "outer"), None),
            P(("inner", "outer"), None),
            P(("inner", "outer"), None),
            P(None, ("inner", "outer")),
            P(),
            P(("inner", "outer"), None),
        ),
        out_specs=(
            P(("inner", "outer"), None),
            P(("inner", "outer"), None),
            P(("inner", "outer"), None),
        ),
        check_vma=False,
    )
```

```python
import functools
import math

import jax
import jax.numpy as jnp
from jax import lax
from jax.experimental import pallas as pl
from jax.experimental.pallas import tpu as pltpu
from jax.sharding import PartitionSpec as P

WINDOW_PATH = ((0, 0), (1, 0), (2, 0), (2, 1), (3, 1), (4, 1), (4, 2))
MESH = pl.DeviceIdType.MESH
LOG2_E = math.log2(math.e)


def kernel(inner_count, outer_count, q_hbm, k_hbm, v_hbm, do_hbm, o_hbm, lse_hbm, span_hbm, code_hbm,
           dq_ref, dk_ref, dv_ref,
           lse_ref, span_ref, code_ref, q_vm, do_vm, o_vm, meta, kv, g_out, g_in, dq_acc, dq_out, dq_in, own_acc,
           load_sem, kv_send, kv_recv, g_send, g_recv, pair_send, pair_recv):
    inner_at = lax.axis_index("inner")
    outer_at = lax.axis_index("outer")
    odd = lax.rem(inner_at, 2)
    is_even, is_odd = odd == 0, odd == 1
    outer_odd = lax.rem(outer_at, 2)
    _, head_count, rows, width = q_vm.shape
    half = rows // 2
    scale = width ** (-0.5)
    steps = len(WINDOW_PATH)
    first_code = 2 * head_count

    def pick(even, other):
        return even if even == other else even + odd * (other - even)

    def shifted(a, c):
        return lax.rem(inner_at + a, inner_count), lax.rem(outer_at + c, outer_count)

    def later(step, other=None):
        a, c = WINDOW_PATH[step]
        d, e = WINDOW_PATH[step if other is None else other]
        return shifted(pick(a % inner_count, d % inner_count), pick(c % outer_count, e % outer_count))

    def earlier(step, other=None):
        a, c = WINDOW_PATH[step]
        d, e = WINDOW_PATH[step if other is None else other]
        return shifted(pick(-a % inner_count, -d % inner_count), pick(-c % outer_count, -e % outer_count))

    mate = (inner_at + 1 - 2 * odd, outer_at)

    barrier = pltpu.get_barrier_semaphore()

    def greet(device):
        pl.semaphore_signal(barrier, inc=1, device_id=device, device_id_type=MESH)

    ahead = shifted(pick(-1 % inner_count, 2 % inner_count), 0)
    for device in (earlier(5), earlier(6), ahead, earlier(2, 4)):
        greet(device)
    greet(mate)
    loads = []

    def load(src, dst, slot):
        copy = pltpu.make_async_copy(src, dst, load_sem.at[slot])
        copy.start()
        loads.append(copy)

    load(k_hbm, kv.at[0, 0], 0)
    load(v_hbm, kv.at[0, 1], 1)
    load(lse_hbm, lse_ref, 2 + 3 * head_count)
    load(span_hbm, span_ref, 3 + 3 * head_count)
    load(code_hbm, code_ref, 4 + 3 * head_count)
    for h in range(head_count):
        columns = pl.ds(h * width, width)
        load(q_hbm.at[:, columns], q_vm.at[0, h], 2 + 3 * h)
        load(do_hbm.at[:, columns], do_vm.at[0, h], 3 + 3 * h)
        load(o_hbm.at[:, columns], o_vm.at[h], 4 + 3 * h)
    for copy in loads[:2]:
        copy.wait()

    pl.semaphore_wait(barrier, 5)

    def remote(src, dst, send_sem, recv_sem, device):
        return pltpu.make_async_remote_copy(
            src_ref=src, dst_ref=dst, send_sem=send_sem, recv_sem=recv_sem,
            device_id=device, device_id_type=MESH)

    def kv_copy(slot, device, source=0, to=None):
        to = slot if to is None else to
        return [remote(kv.at[source, part], kv.at[to, part], kv_send.at[slot - 1, part], kv_recv.at[to - 1, part], device)
                for part in range(2)]

    def wait_kv(slot, part):
        remote(kv.at[0, part], kv.at[slot, part], kv_send.at[slot - 1, part], kv_recv.at[slot - 1, part], mate).wait_recv()

    def begin(copies):
        for copy in copies:
            copy.start()

    def done(copies):
        for copy in copies:
            copy.wait_send()

    def pair_copy(src, dst, slot):
        return remote(src, dst, pair_send.at[slot], pair_recv.at[slot], mate)

    kv_sends = (kv_copy(pick(2, 1), later(2, 1)), kv_copy(6, later(6)), kv_copy(pick(4, 5), later(4, 5)))
    kv_even = kv_copy(5, later(5))
    relay = kv_copy(3, earlier(2), 5)
    begin(kv_sends[0])

    @pl.when(outer_odd == 0)
    def _():
        begin(kv_sends[1])

    for part in range(2):
        kv_sends[2][part].start()
        pl.when(is_even)(kv_even[part].start)

    @pl.when(outer_odd == 1)
    def _():
        begin(kv_sends[1])

    for copy in loads[2:]:
        copy.wait()
    pairs = (pair_copy(q_vm.at[0], q_vm.at[1], 0), pair_copy(do_vm.at[0], do_vm.at[1], 1),
             pair_copy(meta.at[0], meta.at[1], 2))
    dq_pair = tuple(pair_copy(dq_out.at[at], dq_in.at[at], 3 + at) for at in range(2))
    pairs[0].start()
    pairs[1].start()
    meta[0, pl.ds(0, head_count), :] = lse_ref[...] * LOG2_E
    for h in range(head_count):
        product = do_vm[0, h].astype(jnp.float32) * o_vm[h].astype(jnp.float32)
        meta[0, pl.ds(head_count + h, 1), :] = jnp.sum(product.T, axis=0, keepdims=True)
    for at in range(steps - 1):
        meta[0, pl.ds(first_code + at, 1), :] = jnp.full((1, rows), code_ref[0, at].astype(jnp.float32))
    pairs[2].start()

    def g_copy(slot, part, device):
        return remote(g_out.at[slot - 1, part], g_in.at[slot - 1, part], g_send.at[slot - 1, part], g_recv.at[slot - 1, part], device)

    def position(device, shape, dim):
        u, w = device
        block = u * outer_count + w
        first, second = span_ref[2 * block], span_ref[2 * block + 1]
        at = lax.broadcasted_iota(jnp.int32, shape, dim)
        return jnp.where(at < half, first * half + at, second * half + at - half)

    features = head_count * rows

    def dot(x, y, dims):
        return lax.dot_general(x, y, (dims, ((), ())), preferred_element_type=jnp.float32)

    def reach(own, code_step):
        query_pos = position((inner_at, outer_at) if own == 0 else mate, (1, rows), 1)
        if code_step == 0:
            return query_pos
        row = first_code - 1 + (pick(5, 3) if code_step is None else code_step)
        code = meta[own, pl.ds(row, 1), :]
        limit = jnp.where(code == 2.0, jnp.int32(2 ** 31 - 1), jnp.int32(-1))
        return jnp.where(code == 1.0, query_pos, limit)

    def visit(slot, key_device, queries, arrive, give):
        arrive(0)
        key_block = kv[slot, 0]
        first, count = queries[0][0], len(queries)
        q_all = q_vm[pl.ds(first, count)].reshape(count * features, width)
        do_all = do_vm[pl.ds(first, count)].reshape(count * features, width)
        key_pos = position(key_device, (rows, rows), 0)
        allowed, lse_rows, delta_rows = [], [], []
        for own, code_step in queries:
            allowed += [key_pos <= reach(own, code_step)] * head_count
            lse_rows += [meta[own, pl.ds(h, 1), :] for h in range(head_count)]
            delta_rows += [meta[own, pl.ds(head_count + h, 1), :] for h in range(head_count)]
        allowed, lse_row, delta_row = (jnp.concatenate(x, axis=1) for x in (allowed, lse_rows, delta_rows))
        scores = dot(key_block, q_all, ((1,), (1,))) * (scale * LOG2_E)
        probs = jnp.where(allowed, jnp.exp2(scores - lse_row), 0.0)
        give(1, dot(probs.astype(jnp.bfloat16), do_all, ((1,), (0,))))
        arrive(1)
        dprob = dot(kv[slot, 1], do_all, ((1,), (1,)))
        dscore = (probs * (dprob - delta_row)).astype(jnp.bfloat16)
        give(0, dot(dscore, q_all, ((1,), (0,))))
        query_part = dot(key_block.T, dscore, ((1,), (0,)))
        for at, (own, _) in enumerate(queries):
            dq_acc[own] += query_part[:, at * features:(at + 1) * features]

    def send_g(slot, device):
        def give(part, value):
            g_out[slot - 1, part] = (value if part else value * scale).astype(jnp.bfloat16)
            g_copy(slot, part, device).start()

        return give

    def come(slot):
        return lambda part: wait_kv(slot, part)

    def keep(part, value):
        own_acc[part] = value

    def add(part, value):
        own_acc[part] += value

    def nothing(part):
        pass

    dq_acc[...] = jnp.zeros_like(dq_acc)
    visit(0, (inner_at, outer_at), ((0, 0),), nothing, keep)
    for copy in pairs:
        copy.wait_recv()
    def send_dq():
        for at, copy in enumerate(dq_pair):
            dq_out[at] = (dq_acc[1, :, pl.ds(at * features // 2, features // 2)] * scale).astype(jnp.bfloat16)
            copy.start()

    @pl.when(is_even)
    def _():
        visit(0, (inner_at, outer_at), ((1, 1),), nothing, add)
        visit(1, earlier(1), ((0, 1), (1, 2)), come(1), send_g(1, earlier(1)))
        send_dq()
        visit(2, earlier(2), ((0, 2),), come(2), send_g(2, earlier(2)))

    def last_step():
        visit(6, earlier(6), ((0, 6),), come(6), send_g(6, earlier(6)))

    pl.when(outer_odd == 0)(last_step)

    def hand_on(part):
        wait_kv(5, part)
        relay[part].start()

    @pl.when(is_odd)
    def _():
        visit(5, earlier(5), ((0, 5), (1, 4)), hand_on, send_g(5, earlier(5)))
        visit(4, earlier(4), ((0, 4), (1, 3)), come(4), send_g(4, earlier(4)))
        send_dq()

    near = pick(5, 3)
    visit(near, earlier(5, 3), ((0, None),), come(near), send_g(near, earlier(5, 3)))
    pl.when(outer_odd == 1)(last_step)

    for h in range(head_count):
        at, place = divmod(h, head_count // 2)
        if place == 0:
            dq_pair[at].wait_recv()
        part = dq_in[at, :, pl.ds(place * rows, rows)].astype(jnp.float32)
        total = dq_acc[0, :, pl.ds(h * rows, rows)] * scale + part
        dq_ref[:, pl.ds(h * width, width)] = total.T.astype(jnp.bfloat16)

    upper = pick(4, 3)
    last = (pick(2, 1), 6 - outer_odd, 5 + outer_odd * (upper - 5), upper + outer_odd * (6 - upper))
    own_acc[0] *= scale
    for slot in last[:-1]:
        for part in (1, 0):
            g_copy(slot, part, mate).wait_recv()
        own_acc[...] += g_in[slot - 1].astype(jnp.float32)
    for part, out in ((1, dv_ref), (0, dk_ref)):
        g_copy(last[-1], part, mate).wait_recv()
        out[...] = (own_acc[part] + g_in[last[-1] - 1, part].astype(jnp.float32)).astype(jnp.bfloat16)

    for copy in pairs + dq_pair:
        copy.wait_send()
    for copies in kv_sends:
        done(copies)
    pl.when(is_even)(functools.partial(done, kv_even))
    pl.when(is_odd)(functools.partial(done, relay))
    for slot in (pick(1, 4), pick(2, 3), 5, 6):
        for part in range(2):
            g_copy(slot, part, mate).wait_send()


def finish(dq_in, dk_in, dv_in, dq_out, dk_out, dv_out, sems):
    moves = [pltpu.make_async_copy(src, dst, sems.at[slot])
             for slot, (src, dst) in enumerate(((dq_in, dq_out), (dk_in, dk_out), (dv_in, dv_out)))]
    for move in moves:
        move.start()
    for move in moves:
        move.wait()


def shards(queries, keys, values, out_grad, forward_out, log_sum_exp, span_table, mask_codes):
    rows, features = queries.shape
    width = keys.shape[1]
    heads = log_sum_exp.shape[0]
    remote = len(WINDOW_PATH) - 1
    hbm = pl.BlockSpec(memory_space=pl.ANY)
    vmem = pl.BlockSpec(memory_space=pltpu.VMEM)
    grads = (
        jax.ShapeDtypeStruct((rows, features), jnp.bfloat16),
        jax.ShapeDtypeStruct((rows, width), jnp.bfloat16),
        jax.ShapeDtypeStruct((rows, width), jnp.bfloat16),
    )
    parts = pl.pallas_call(
        functools.partial(kernel, lax.axis_size("inner"), lax.axis_size("outer")),
        out_shape=grads,
        in_specs=[hbm] * 8,
        out_specs=(vmem, vmem, vmem),
        scratch_shapes=[
            pltpu.VMEM((heads, rows), jnp.float32),
            pltpu.SMEM(span_table.shape, jnp.int32),
            pltpu.SMEM(mask_codes.shape, jnp.int32),
            pltpu.VMEM((2, heads, rows, width), jnp.bfloat16),
            pltpu.VMEM((2, heads, rows, width), jnp.bfloat16),
            pltpu.VMEM((heads, rows, width), jnp.bfloat16),
            pltpu.VMEM((2, 2 * heads + 8, rows), jnp.float32),
            pltpu.VMEM((1 + remote, 2, rows, width), jnp.bfloat16),
            pltpu.VMEM((remote, 2, rows, width), jnp.bfloat16),
            pltpu.VMEM((remote, 2, rows, width), jnp.bfloat16),
            pltpu.VMEM((2, width, heads * rows), jnp.float32),
            pltpu.VMEM((2, width, heads * rows // 2), jnp.bfloat16),
            pltpu.VMEM((2, width, heads * rows // 2), jnp.bfloat16),
            pltpu.VMEM((2, rows, width), jnp.float32),
            pltpu.SemaphoreType.DMA((5 + 3 * heads,)),
            pltpu.SemaphoreType.DMA((remote, 2)),
            pltpu.SemaphoreType.DMA((remote, 2)),
            pltpu.SemaphoreType.DMA((remote, 2)),
            pltpu.SemaphoreType.DMA((remote, 2)),
            pltpu.SemaphoreType.DMA((5,)),
            pltpu.SemaphoreType.DMA((5,)),
        ],
        compiler_params=pltpu.CompilerParams(
            collective_id=0, has_side_effects=True, vmem_limit_bytes=16 * 2 ** 20),
    )(*(pltpu.with_memory_space_constraint(x, pltpu.HBM) for x in (queries, keys, values, out_grad, forward_out, log_sum_exp, span_table, mask_codes)))
    return pl.pallas_call(
        finish,
        out_shape=grads,
        in_specs=[hbm] * 3,
        out_specs=(hbm, hbm, hbm),
        scratch_shapes=[pltpu.SemaphoreType.DMA((3,))],
        compiler_params=pltpu.CompilerParams(vmem_limit_bytes=2 ** 20),
    )(*parts)


def solution(mesh):
    return jax.shard_map(
        shards,
        mesh=mesh,
        in_specs=(
            P(("inner", "outer"), None),
            P(("inner", "outer"), None),
            P(("inner", "outer"), None),
            P(("inner", "outer"), None),
            P(("inner", "outer"), None),
            P(None, ("inner", "outer")),
            P(),
            P(("inner", "outer"), None),
        ),
        out_specs=(
            P(("inner", "outer"), None),
            P(("inner", "outer"), None),
            P(("inner", "outer"), None),
        ),
        check_vma=False,
    )
```

```python
import functools
import math

import jax
import jax.numpy as jnp
from jax import lax
from jax.experimental import pallas as pl
from jax.experimental.pallas import tpu as pltpu
from jax.sharding import PartitionSpec as P

WINDOW_PATH = ((0, 0), (1, 0), (2, 0), (2, 1), (3, 1), (4, 1), (4, 2))
MESH = pl.DeviceIdType.MESH
LOG2_E = math.log2(math.e)


def kernel(inner_count, outer_count, q_hbm, k_hbm, v_hbm, do_hbm, o_hbm, lse_hbm, span_hbm, code_hbm,
           dq_ref, dk_ref, dv_ref,
           lse_ref, span_ref, code_ref, q_vm, do_vm, o_vm, meta, kv, g_out, g_in, dq_acc, dq_out, dq_in, own_acc,
           load_sem, kv_send, kv_recv, g_send, g_recv, pair_send, pair_recv):
    inner_at = lax.axis_index("inner")
    outer_at = lax.axis_index("outer")
    odd = lax.rem(inner_at, 2)
    is_even, is_odd = odd == 0, odd == 1
    outer_odd = lax.rem(outer_at, 2)
    _, head_count, rows, width = q_vm.shape
    half = rows // 2
    scale = width ** (-0.5)
    steps = len(WINDOW_PATH)
    first_code = 2 * head_count

    def pick(even, other):
        return even if even == other else even + odd * (other - even)

    def shifted(a, c):
        return lax.rem(inner_at + a, inner_count), lax.rem(outer_at + c, outer_count)

    def later(step, other=None):
        a, c = WINDOW_PATH[step]
        d, e = WINDOW_PATH[step if other is None else other]
        return shifted(pick(a % inner_count, d % inner_count), pick(c % outer_count, e % outer_count))

    def earlier(step, other=None):
        a, c = WINDOW_PATH[step]
        d, e = WINDOW_PATH[step if other is None else other]
        return shifted(pick(-a % inner_count, -d % inner_count), pick(-c % outer_count, -e % outer_count))

    mate = (inner_at + 1 - 2 * odd, outer_at)

    loads = []

    def load(src, dst, slot):
        copy = pltpu.make_async_copy(src, dst, load_sem.at[slot])
        copy.start()
        loads.append(copy)

    load(k_hbm, kv.at[0, 0], 0)
    load(v_hbm, kv.at[0, 1], 1)
    barrier = pltpu.get_barrier_semaphore()

    def greet(device):
        pl.semaphore_signal(barrier, inc=1, device_id=device, device_id_type=MESH)

    ahead = shifted(pick(-1 % inner_count, 2 % inner_count), 0)
    for device in (earlier(5), earlier(6), ahead, earlier(2, 4)):
        greet(device)
    greet(mate)
    load(lse_hbm, lse_ref, 2 + 3 * head_count)
    load(span_hbm, span_ref, 3 + 3 * head_count)
    load(code_hbm, code_ref, 4 + 3 * head_count)
    for h in range(head_count):
        columns = pl.ds(h * width, width)
        load(q_hbm.at[:, columns], q_vm.at[0, h], 2 + 3 * h)
        load(do_hbm.at[:, columns], do_vm.at[0, h], 3 + 3 * h)
        load(o_hbm.at[:, columns], o_vm.at[h], 4 + 3 * h)
    for copy in loads[:2]:
        copy.wait()

    pl.semaphore_wait(barrier, 5)

    def remote(src, dst, send_sem, recv_sem, device):
        return pltpu.make_async_remote_copy(
            src_ref=src, dst_ref=dst, send_sem=send_sem, recv_sem=recv_sem,
            device_id=device, device_id_type=MESH)

    def kv_copy(slot, device, source=0, to=None):
        to = slot if to is None else to
        return [remote(kv.at[source, part], kv.at[to, part], kv_send.at[slot - 1, part], kv_recv.at[to - 1, part], device)
                for part in range(2)]

    def wait_kv(slot, part):
        remote(kv.at[0, part], kv.at[slot, part], kv_send.at[slot - 1, part], kv_recv.at[slot - 1, part], mate).wait_recv()

    def begin(copies):
        for copy in copies:
            copy.start()

    def done(copies):
        for copy in copies:
            copy.wait_send()

    def pair_copy(src, dst, slot):
        return remote(src, dst, pair_send.at[slot], pair_recv.at[slot], mate)

    kv_sends = (kv_copy(pick(2, 1), later(2, 1)), kv_copy(6, later(6)), kv_copy(pick(4, 5), later(4, 5)))
    kv_even = kv_copy(5, later(5))
    relay = kv_copy(3, earlier(2), 5)
    @pl.when(outer_odd == 0)
    def _():
        begin(kv_sends[0])
        begin(kv_sends[1])

    for part in range(2):
        kv_sends[2][part].start()
        pl.when(is_even)(kv_even[part].start)

    @pl.when(outer_odd == 1)
    def _():
        begin(kv_sends[0])
        begin(kv_sends[1])

    for copy in loads[2:]:
        copy.wait()
    pairs = (pair_copy(q_vm.at[0], q_vm.at[1], 0), pair_copy(do_vm.at[0], do_vm.at[1], 1),
             pair_copy(meta.at[0], meta.at[1], 2))
    dq_pair = tuple(pair_copy(dq_out.at[at], dq_in.at[at], 3 + at) for at in range(2))
    pairs[0].start()
    pairs[1].start()
    meta[0, pl.ds(0, head_count), :] = lse_ref[...] * LOG2_E
    for h in range(head_count):
        product = do_vm[0, h].astype(jnp.float32) * o_vm[h].astype(jnp.float32)
        meta[0, pl.ds(head_count + h, 1), :] = jnp.sum(product.T, axis=0, keepdims=True)
    for at in range(steps - 1):
        meta[0, pl.ds(first_code + at, 1), :] = jnp.full((1, rows), code_ref[0, at].astype(jnp.float32))
    pairs[2].start()

    def g_copy(slot, part, device):
        return remote(g_out.at[slot - 1, part], g_in.at[slot - 1, part], g_send.at[slot - 1, part], g_recv.at[slot - 1, part], device)

    def position(device, shape, dim):
        u, w = device
        block = u * outer_count + w
        first, second = span_ref[2 * block], span_ref[2 * block + 1]
        at = lax.broadcasted_iota(jnp.int32, shape, dim)
        return jnp.where(at < half, first * half + at, second * half + at - half)

    features = head_count * rows

    def dot(x, y, dims):
        return lax.dot_general(x, y, (dims, ((), ())), preferred_element_type=jnp.float32)

    def reach(own, code_step):
        query_pos = position((inner_at, outer_at) if own == 0 else mate, (1, rows), 1)
        if code_step == 0:
            return query_pos
        row = first_code - 1 + (pick(5, 3) if code_step is None else code_step)
        code = meta[own, pl.ds(row, 1), :]
        limit = jnp.where(code == 2.0, jnp.int32(2 ** 31 - 1), jnp.int32(-1))
        return jnp.where(code == 1.0, query_pos, limit)

    def visit(slot, key_device, queries, arrive, give):
        arrive(0)
        key_block = kv[slot, 0]
        first, count = queries[0][0], len(queries)
        q_all = q_vm[pl.ds(first, count)].reshape(count * features, width)
        do_all = do_vm[pl.ds(first, count)].reshape(count * features, width)
        key_pos = position(key_device, (rows, rows), 0)
        allowed, lse_rows, delta_rows = [], [], []
        for own, code_step in queries:
            allowed += [key_pos <= reach(own, code_step)] * head_count
            lse_rows += [meta[own, pl.ds(h, 1), :] for h in range(head_count)]
            delta_rows += [meta[own, pl.ds(head_count + h, 1), :] for h in range(head_count)]
        allowed, lse_row, delta_row = (jnp.concatenate(x, axis=1) for x in (allowed, lse_rows, delta_rows))
        scores = dot(key_block, q_all, ((1,), (1,))) * (scale * LOG2_E)
        probs = jnp.where(allowed, jnp.exp2(scores - lse_row), 0.0)
        give(1, dot(probs.astype(jnp.bfloat16), do_all, ((1,), (0,))))
        arrive(1)
        dprob = dot(kv[slot, 1], do_all, ((1,), (1,)))
        dscore = (probs * (dprob - delta_row)).astype(jnp.bfloat16)
        give(0, dot(dscore, q_all, ((1,), (0,))))
        query_part = dot(key_block.T, dscore, ((1,), (0,)))
        for at, (own, _) in enumerate(queries):
            dq_acc[own] += query_part[:, at * features:(at + 1) * features]

    def send_g(slot, device):
        def give(part, value):
            g_out[slot - 1, part] = (value if part else value * scale).astype(jnp.bfloat16)
            g_copy(slot, part, device).start()

        return give

    def come(slot):
        return lambda part: wait_kv(slot, part)

    def keep(part, value):
        own_acc[part] = value

    def add(part, value):
        own_acc[part] += value

    def nothing(part):
        pass

    dq_acc[...] = jnp.zeros_like(dq_acc)
    visit(0, (inner_at, outer_at), ((0, 0),), nothing, keep)
    for copy in pairs:
        copy.wait_recv()
    def send_dq():
        for at, copy in enumerate(dq_pair):
            dq_out[at] = (dq_acc[1, :, pl.ds(at * features // 2, features // 2)] * scale).astype(jnp.bfloat16)
            copy.start()

    @pl.when(is_even)
    def _():
        visit(0, (inner_at, outer_at), ((1, 1),), nothing, add)
        visit(1, earlier(1), ((0, 1), (1, 2)), come(1), send_g(1, earlier(1)))
        send_dq()
        visit(2, earlier(2), ((0, 2),), come(2), send_g(2, earlier(2)))

    def last_step():
        visit(6, earlier(6), ((0, 6),), come(6), send_g(6, earlier(6)))

    pl.when(outer_odd == 0)(last_step)

    def hand_on(part):
        wait_kv(5, part)
        relay[part].start()

    @pl.when(is_odd)
    def _():
        visit(5, earlier(5), ((0, 5), (1, 4)), hand_on, send_g(5, earlier(5)))
        visit(4, earlier(4), ((0, 4), (1, 3)), come(4), send_g(4, earlier(4)))
        send_dq()

    near = pick(5, 3)
    visit(near, earlier(5, 3), ((0, None),), come(near), send_g(near, earlier(5, 3)))
    pl.when(outer_odd == 1)(last_step)

    for h in range(head_count):
        at, place = divmod(h, head_count // 2)
        if place == 0:
            dq_pair[at].wait_recv()
        part = dq_in[at, :, pl.ds(place * rows, rows)].astype(jnp.float32)
        total = dq_acc[0, :, pl.ds(h * rows, rows)] * scale + part
        dq_ref[:, pl.ds(h * width, width)] = total.T.astype(jnp.bfloat16)

    upper = pick(4, 3)
    last = (pick(2, 1), 6 - outer_odd, 5 + outer_odd * (upper - 5), upper + outer_odd * (6 - upper))
    own_acc[0] *= scale
    for slot in last[:-1]:
        for part in (1, 0):
            g_copy(slot, part, mate).wait_recv()
        own_acc[...] += g_in[slot - 1].astype(jnp.float32)
    for part, out in ((1, dv_ref), (0, dk_ref)):
        g_copy(last[-1], part, mate).wait_recv()
        out[...] = (own_acc[part] + g_in[last[-1] - 1, part].astype(jnp.float32)).astype(jnp.bfloat16)

    for copy in pairs + dq_pair:
        copy.wait_send()
    for copies in kv_sends:
        done(copies)
    pl.when(is_even)(functools.partial(done, kv_even))
    pl.when(is_odd)(functools.partial(done, relay))
    for slot in (pick(1, 4), pick(2, 3), 5, 6):
        for part in range(2):
            g_copy(slot, part, mate).wait_send()


def finish(dq_in, dk_in, dv_in, dq_out, dk_out, dv_out, sems):
    moves = [pltpu.make_async_copy(src, dst, sems.at[slot])
             for slot, (src, dst) in enumerate(((dq_in, dq_out), (dk_in, dk_out), (dv_in, dv_out)))]
    for move in moves:
        move.start()
    for move in moves:
        move.wait()


def shards(queries, keys, values, out_grad, forward_out, log_sum_exp, span_table, mask_codes):
    rows, features = queries.shape
    width = keys.shape[1]
    heads = log_sum_exp.shape[0]
    remote = len(WINDOW_PATH) - 1
    hbm = pl.BlockSpec(memory_space=pl.ANY)
    vmem = pl.BlockSpec(memory_space=pltpu.VMEM)
    grads = (
        jax.ShapeDtypeStruct((rows, features), jnp.bfloat16),
        jax.ShapeDtypeStruct((rows, width), jnp.bfloat16),
        jax.ShapeDtypeStruct((rows, width), jnp.bfloat16),
    )
    parts = pl.pallas_call(
        functools.partial(kernel, lax.axis_size("inner"), lax.axis_size("outer")),
        out_shape=grads,
        in_specs=[hbm] * 8,
        out_specs=(vmem, vmem, vmem),
        scratch_shapes=[
            pltpu.VMEM((heads, rows), jnp.float32),
            pltpu.SMEM(span_table.shape, jnp.int32),
            pltpu.SMEM(mask_codes.shape, jnp.int32),
            pltpu.VMEM((2, heads, rows, width), jnp.bfloat16),
            pltpu.VMEM((2, heads, rows, width), jnp.bfloat16),
            pltpu.VMEM((heads, rows, width), jnp.bfloat16),
            pltpu.VMEM((2, 2 * heads + 8, rows), jnp.float32),
            pltpu.VMEM((1 + remote, 2, rows, width), jnp.bfloat16),
            pltpu.VMEM((remote, 2, rows, width), jnp.bfloat16),
            pltpu.VMEM((remote, 2, rows, width), jnp.bfloat16),
            pltpu.VMEM((2, width, heads * rows), jnp.float32),
            pltpu.VMEM((2, width, heads * rows // 2), jnp.bfloat16),
            pltpu.VMEM((2, width, heads * rows // 2), jnp.bfloat16),
            pltpu.VMEM((2, rows, width), jnp.float32),
            pltpu.SemaphoreType.DMA((5 + 3 * heads,)),
            pltpu.SemaphoreType.DMA((remote, 2)),
            pltpu.SemaphoreType.DMA((remote, 2)),
            pltpu.SemaphoreType.DMA((remote, 2)),
            pltpu.SemaphoreType.DMA((remote, 2)),
            pltpu.SemaphoreType.DMA((5,)),
            pltpu.SemaphoreType.DMA((5,)),
        ],
        compiler_params=pltpu.CompilerParams(
            collective_id=0, has_side_effects=True, vmem_limit_bytes=16 * 2 ** 20),
    )(*(pltpu.with_memory_space_constraint(x, pltpu.HBM) for x in (queries, keys, values, out_grad, forward_out, log_sum_exp, span_table, mask_codes)))
    return pl.pallas_call(
        finish,
        out_shape=grads,
        in_specs=[hbm] * 3,
        out_specs=(hbm, hbm, hbm),
        scratch_shapes=[pltpu.SemaphoreType.DMA((3,))],
        compiler_params=pltpu.CompilerParams(vmem_limit_bytes=2 ** 20),
    )(*parts)


def solution(mesh):
    return jax.shard_map(
        shards,
        mesh=mesh,
        in_specs=(
            P(("inner", "outer"), None),
            P(("inner", "outer"), None),
            P(("inner", "outer"), None),
            P(("inner", "outer"), None),
            P(("inner", "outer"), None),
            P(None, ("inner", "outer")),
            P(),
            P(("inner", "outer"), None),
        ),
        out_specs=(
            P(("inner", "outer"), None),
            P(("inner", "outer"), None),
            P(("inner", "outer"), None),
        ),
        check_vma=False,
    )
```

```python
import functools
import math

import jax
import jax.numpy as jnp
from jax import lax
from jax.experimental import pallas as pl
from jax.experimental.pallas import tpu as pltpu
from jax.sharding import PartitionSpec as P

WINDOW_PATH = ((0, 0), (1, 0), (2, 0), (2, 1), (3, 1), (4, 1), (4, 2))
MESH = pl.DeviceIdType.MESH
LOG2_E = math.log2(math.e)


def kernel(inner_count, outer_count, q_hbm, k_hbm, v_hbm, do_hbm, o_hbm, lse_hbm, span_hbm, code_hbm,
           dq_ref, dk_ref, dv_ref,
           lse_ref, span_ref, code_ref, q_vm, do_vm, o_vm, meta, kv, g_out, g_in, dq_acc, dq_out, dq_in, own_acc,
           load_sem, kv_send, kv_recv, g_send, g_recv, pair_send, pair_recv):
    inner_at = lax.axis_index("inner")
    outer_at = lax.axis_index("outer")
    odd = lax.rem(inner_at, 2)
    is_even, is_odd = odd == 0, odd == 1
    outer_odd = lax.rem(outer_at, 2)
    _, head_count, rows, width = q_vm.shape
    half = rows // 2
    scale = width ** (-0.5)
    steps = len(WINDOW_PATH)
    first_code = 2 * head_count

    def pick(even, other):
        return even if even == other else even + odd * (other - even)

    def shifted(a, c):
        return lax.rem(inner_at + a, inner_count), lax.rem(outer_at + c, outer_count)

    def later(step, other=None):
        a, c = WINDOW_PATH[step]
        d, e = WINDOW_PATH[step if other is None else other]
        return shifted(pick(a % inner_count, d % inner_count), pick(c % outer_count, e % outer_count))

    def earlier(step, other=None):
        a, c = WINDOW_PATH[step]
        d, e = WINDOW_PATH[step if other is None else other]
        return shifted(pick(-a % inner_count, -d % inner_count), pick(-c % outer_count, -e % outer_count))

    mate = (inner_at + 1 - 2 * odd, outer_at)

    loads = []

    def load(src, dst, slot):
        copy = pltpu.make_async_copy(src, dst, load_sem.at[slot])
        copy.start()
        loads.append(copy)

    load(k_hbm, kv.at[0, 0], 0)
    load(v_hbm, kv.at[0, 1], 1)
    barrier = pltpu.get_barrier_semaphore()

    def greet(device):
        pl.semaphore_signal(barrier, inc=1, device_id=device, device_id_type=MESH)

    ahead = shifted(pick(-1 % inner_count, 2 % inner_count), 0)
    for device in (earlier(5), earlier(6), ahead, earlier(2, 4)):
        greet(device)
    greet(mate)
    load(lse_hbm, lse_ref, 2 + 3 * head_count)
    load(span_hbm, span_ref, 3 + 3 * head_count)
    load(code_hbm, code_ref, 4 + 3 * head_count)
    for h in range(head_count):
        columns = pl.ds(h * width, width)
        load(q_hbm.at[:, columns], q_vm.at[0, h], 2 + 3 * h)
        load(do_hbm.at[:, columns], do_vm.at[0, h], 3 + 3 * h)
        load(o_hbm.at[:, columns], o_vm.at[h], 4 + 3 * h)
    for copy in loads[:2]:
        copy.wait()

    pl.semaphore_wait(barrier, 5)

    def remote(src, dst, send_sem, recv_sem, device):
        return pltpu.make_async_remote_copy(
            src_ref=src, dst_ref=dst, send_sem=send_sem, recv_sem=recv_sem,
            device_id=device, device_id_type=MESH)

    def kv_copy(slot, device, source=0, to=None):
        to = slot if to is None else to
        return [remote(kv.at[source, part], kv.at[to, part], kv_send.at[slot - 1, part], kv_recv.at[to - 1, part], device)
                for part in range(2)]

    def wait_kv(slot, part):
        remote(kv.at[0, part], kv.at[slot, part], kv_send.at[slot - 1, part], kv_recv.at[slot - 1, part], mate).wait_recv()

    def begin(copies):
        for copy in copies:
            copy.start()

    def done(copies):
        for copy in copies:
            copy.wait_send()

    def pair_copy(src, dst, slot):
        return remote(src, dst, pair_send.at[slot], pair_recv.at[slot], mate)

    kv_sends = (kv_copy(pick(2, 1), later(2, 1)), kv_copy(6, later(6)), kv_copy(pick(4, 5), later(4, 5)))
    kv_even = kv_copy(5, later(5))
    relay = kv_copy(3, earlier(2), 5)
    @pl.when(outer_odd == 0)
    def _():
        begin(kv_sends[0])
        begin(kv_sends[1])

    for part in range(2):
        kv_sends[2][part].start()
        pl.when(is_even)(kv_even[part].start)

    @pl.when(outer_odd == 1)
    def _():
        begin(kv_sends[0])
        begin(kv_sends[1])

    for copy in loads[2:]:
        copy.wait()
    pairs = (pair_copy(q_vm.at[0], q_vm.at[1], 0), pair_copy(do_vm.at[0], do_vm.at[1], 1),
             pair_copy(meta.at[0], meta.at[1], 2))
    dq_pair = tuple(pair_copy(dq_out.at[at], dq_in.at[at], 3 + at) for at in range(2))
    pairs[0].start()
    pairs[1].start()
    meta[0, pl.ds(0, head_count), :] = lse_ref[...] * LOG2_E
    for h in range(head_count):
        product = do_vm[0, h].astype(jnp.float32) * o_vm[h].astype(jnp.float32)
        meta[0, pl.ds(head_count + h, 1), :] = jnp.sum(product.T, axis=0, keepdims=True)
    for at in range(steps - 1):
        meta[0, pl.ds(first_code + at, 1), :] = jnp.full((1, rows), code_ref[0, at].astype(jnp.float32))
    pairs[2].start()

    def g_copy(slot, part, device):
        return remote(g_out.at[slot - 1, part], g_in.at[slot - 1, part], g_send.at[slot - 1, part], g_recv.at[slot - 1, part], device)

    def position(device, shape, dim):
        u, w = device
        block = u * outer_count + w
        first, second = span_ref[2 * block], span_ref[2 * block + 1]
        at = lax.broadcasted_iota(jnp.int32, shape, dim)
        return jnp.where(at < half, first * half + at, second * half + at - half)

    features = head_count * rows

    def dot(x, y, dims):
        return lax.dot_general(x, y, (dims, ((), ())), preferred_element_type=jnp.float32)

    def reach(own, code_step):
        query_pos = position((inner_at, outer_at) if own == 0 else mate, (1, rows), 1)
        if code_step == 0:
            return query_pos
        row = first_code - 1 + (pick(5, 3) if code_step is None else code_step)
        code = meta[own, pl.ds(row, 1), :]
        limit = jnp.where(code == 2.0, jnp.int32(2 ** 31 - 1), jnp.int32(-1))
        return jnp.where(code == 1.0, query_pos, limit)

    def visit(slot, key_device, queries, arrive, give):
        arrive(0)
        key_block = kv[slot, 0]
        first, count = queries[0][0], len(queries)
        q_all = q_vm[pl.ds(first, count)].reshape(count * features, width)
        do_all = do_vm[pl.ds(first, count)].reshape(count * features, width)
        key_pos = position(key_device, (rows, rows), 0)
        allowed, lse_rows, delta_rows = [], [], []
        for own, code_step in queries:
            allowed += [key_pos <= reach(own, code_step)] * head_count
            lse_rows += [meta[own, pl.ds(h, 1), :] for h in range(head_count)]
            delta_rows += [meta[own, pl.ds(head_count + h, 1), :] for h in range(head_count)]
        allowed, lse_row, delta_row = (jnp.concatenate(x, axis=1) for x in (allowed, lse_rows, delta_rows))
        scores = dot(key_block, q_all, ((1,), (1,))) * (scale * LOG2_E)
        probs = jnp.where(allowed, jnp.exp2(scores - lse_row), 0.0)
        give(1, dot(probs.astype(jnp.bfloat16), do_all, ((1,), (0,))))
        arrive(1)
        dprob = dot(kv[slot, 1], do_all, ((1,), (1,)))
        dscore = (probs * (dprob - delta_row) * scale).astype(jnp.bfloat16)
        give(0, dot(dscore, q_all, ((1,), (0,))))
        query_part = dot(key_block.T, dscore, ((1,), (0,)))
        for at, (own, _) in enumerate(queries):
            dq_acc[own] += query_part[:, at * features:(at + 1) * features]

    def send_g(slot, device):
        def give(part, value):
            g_out[slot - 1, part] = value.astype(jnp.bfloat16)
            g_copy(slot, part, device).start()

        return give

    def come(slot):
        return lambda part: wait_kv(slot, part)

    def keep(part, value):
        own_acc[part] = value

    def add(part, value):
        own_acc[part] += value

    def nothing(part):
        pass

    dq_acc[...] = jnp.zeros_like(dq_acc)
    visit(0, (inner_at, outer_at), ((0, 0),), nothing, keep)
    for copy in pairs:
        copy.wait_recv()
    def send_dq():
        for at, copy in enumerate(dq_pair):
            dq_out[at] = dq_acc[1, :, pl.ds(at * features // 2, features // 2)].astype(jnp.bfloat16)
            copy.start()

    @pl.when(is_even)
    def _():
        visit(0, (inner_at, outer_at), ((1, 1),), nothing, add)
        visit(1, earlier(1), ((0, 1), (1, 2)), come(1), send_g(1, earlier(1)))
        send_dq()
        visit(2, earlier(2), ((0, 2),), come(2), send_g(2, earlier(2)))

    def last_step():
        visit(6, earlier(6), ((0, 6),), come(6), send_g(6, earlier(6)))

    pl.when(outer_odd == 0)(last_step)

    def hand_on(part):
        wait_kv(5, part)
        relay[part].start()

    @pl.when(is_odd)
    def _():
        visit(5, earlier(5), ((0, 5), (1, 4)), hand_on, send_g(5, earlier(5)))
        visit(4, earlier(4), ((0, 4), (1, 3)), come(4), send_g(4, earlier(4)))
        send_dq()

    near = pick(5, 3)
    visit(near, earlier(5, 3), ((0, None),), come(near), send_g(near, earlier(5, 3)))
    pl.when(outer_odd == 1)(last_step)

    for h in range(head_count):
        at, place = divmod(h, head_count // 2)
        if place == 0:
            dq_pair[at].wait_recv()
        part = dq_in[at, :, pl.ds(place * rows, rows)].astype(jnp.float32)
        total = dq_acc[0, :, pl.ds(h * rows, rows)] + part
        dq_ref[:, pl.ds(h * width, width)] = total.T.astype(jnp.bfloat16)

    upper = pick(4, 3)
    last = (pick(2, 1), 6 - outer_odd, 5 + outer_odd * (upper - 5), upper + outer_odd * (6 - upper))
    for slot in last[:-1]:
        for part in (1, 0):
            g_copy(slot, part, mate).wait_recv()
        own_acc[...] += g_in[slot - 1].astype(jnp.float32)
    for part, out in ((1, dv_ref), (0, dk_ref)):
        g_copy(last[-1], part, mate).wait_recv()
        out[...] = (own_acc[part] + g_in[last[-1] - 1, part].astype(jnp.float32)).astype(jnp.bfloat16)

    for copy in pairs + dq_pair:
        copy.wait_send()
    for copies in kv_sends:
        done(copies)
    pl.when(is_even)(functools.partial(done, kv_even))
    pl.when(is_odd)(functools.partial(done, relay))
    for slot in (pick(1, 4), pick(2, 3), 5, 6):
        for part in range(2):
            g_copy(slot, part, mate).wait_send()


def finish(dq_in, dk_in, dv_in, dq_out, dk_out, dv_out, sems):
    moves = [pltpu.make_async_copy(src, dst, sems.at[slot])
             for slot, (src, dst) in enumerate(((dq_in, dq_out), (dk_in, dk_out), (dv_in, dv_out)))]
    for move in moves:
        move.start()
    for move in moves:
        move.wait()


def shards(queries, keys, values, out_grad, forward_out, log_sum_exp, span_table, mask_codes):
    rows, features = queries.shape
    width = keys.shape[1]
    heads = log_sum_exp.shape[0]
    remote = len(WINDOW_PATH) - 1
    hbm = pl.BlockSpec(memory_space=pl.ANY)
    vmem = pl.BlockSpec(memory_space=pltpu.VMEM)
    grads = (
        jax.ShapeDtypeStruct((rows, features), jnp.bfloat16),
        jax.ShapeDtypeStruct((rows, width), jnp.bfloat16),
        jax.ShapeDtypeStruct((rows, width), jnp.bfloat16),
    )
    parts = pl.pallas_call(
        functools.partial(kernel, lax.axis_size("inner"), lax.axis_size("outer")),
        out_shape=grads,
        in_specs=[hbm] * 8,
        out_specs=(vmem, vmem, vmem),
        scratch_shapes=[
            pltpu.VMEM((heads, rows), jnp.float32),
            pltpu.SMEM(span_table.shape, jnp.int32),
            pltpu.SMEM(mask_codes.shape, jnp.int32),
            pltpu.VMEM((2, heads, rows, width), jnp.bfloat16),
            pltpu.VMEM((2, heads, rows, width), jnp.bfloat16),
            pltpu.VMEM((heads, rows, width), jnp.bfloat16),
            pltpu.VMEM((2, 2 * heads + 8, rows), jnp.float32),
            pltpu.VMEM((1 + remote, 2, rows, width), jnp.bfloat16),
            pltpu.VMEM((remote, 2, rows, width), jnp.bfloat16),
            pltpu.VMEM((remote, 2, rows, width), jnp.bfloat16),
            pltpu.VMEM((2, width, heads * rows), jnp.float32),
            pltpu.VMEM((2, width, heads * rows // 2), jnp.bfloat16),
            pltpu.VMEM((2, width, heads * rows // 2), jnp.bfloat16),
            pltpu.VMEM((2, rows, width), jnp.float32),
            pltpu.SemaphoreType.DMA((5 + 3 * heads,)),
            pltpu.SemaphoreType.DMA((remote, 2)),
            pltpu.SemaphoreType.DMA((remote, 2)),
            pltpu.SemaphoreType.DMA((remote, 2)),
            pltpu.SemaphoreType.DMA((remote, 2)),
            pltpu.SemaphoreType.DMA((5,)),
            pltpu.SemaphoreType.DMA((5,)),
        ],
        compiler_params=pltpu.CompilerParams(
            collective_id=0, has_side_effects=True, vmem_limit_bytes=16 * 2 ** 20),
    )(*(pltpu.with_memory_space_constraint(x, pltpu.HBM) for x in (queries, keys, values, out_grad, forward_out, log_sum_exp, span_table, mask_codes)))
    return pl.pallas_call(
        finish,
        out_shape=grads,
        in_specs=[hbm] * 3,
        out_specs=(hbm, hbm, hbm),
        scratch_shapes=[pltpu.SemaphoreType.DMA((3,))],
        compiler_params=pltpu.CompilerParams(vmem_limit_bytes=2 ** 20),
    )(*parts)


def solution(mesh):
    return jax.shard_map(
        shards,
        mesh=mesh,
        in_specs=(
            P(("inner", "outer"), None),
            P(("inner", "outer"), None),
            P(("inner", "outer"), None),
            P(("inner", "outer"), None),
            P(("inner", "outer"), None),
            P(None, ("inner", "outer")),
            P(),
            P(("inner", "outer"), None),
        ),
        out_specs=(
            P(("inner", "outer"), None),
            P(("inner", "outer"), None),
            P(("inner", "outer"), None),
        ),
        check_vma=False,
    )
```

```python
import functools
import math

import jax
import jax.numpy as jnp
from jax import lax
from jax.experimental import pallas as pl
from jax.experimental.pallas import tpu as pltpu
from jax.sharding import PartitionSpec as P

WINDOW_PATH = ((0, 0), (1, 0), (2, 0), (2, 1), (3, 1), (4, 1), (4, 2))
MESH = pl.DeviceIdType.MESH
LOG2_E = math.log2(math.e)


def kernel(inner_count, outer_count, q_hbm, k_hbm, v_hbm, do_hbm, o_hbm, lse_hbm, span_hbm, code_hbm,
           dq_ref, dk_ref, dv_ref,
           lse_ref, span_ref, code_ref, q_vm, do_vm, o_vm, meta, kv, g_out, g_in, dq_acc, dq_out, dq_in, own_acc,
           load_sem, kv_send, kv_recv, g_send, g_recv, pair_send, pair_recv):
    inner_at = lax.axis_index("inner")
    outer_at = lax.axis_index("outer")
    odd = lax.rem(inner_at, 2)
    is_even, is_odd = odd == 0, odd == 1
    outer_odd = lax.rem(outer_at, 2)
    _, head_count, rows, width = q_vm.shape
    half = rows // 2
    scale = width ** (-0.5)
    steps = len(WINDOW_PATH)
    first_code = 2 * head_count

    def pick(even, other):
        return even if even == other else even + odd * (other - even)

    def shifted(a, c):
        return lax.rem(inner_at + a, inner_count), lax.rem(outer_at + c, outer_count)

    def later(step, other=None):
        a, c = WINDOW_PATH[step]
        d, e = WINDOW_PATH[step if other is None else other]
        return shifted(pick(a % inner_count, d % inner_count), pick(c % outer_count, e % outer_count))

    def earlier(step, other=None):
        a, c = WINDOW_PATH[step]
        d, e = WINDOW_PATH[step if other is None else other]
        return shifted(pick(-a % inner_count, -d % inner_count), pick(-c % outer_count, -e % outer_count))

    mate = (inner_at + 1 - 2 * odd, outer_at)

    loads = []

    def load(src, dst, slot):
        copy = pltpu.make_async_copy(src, dst, load_sem.at[slot])
        copy.start()
        loads.append(copy)

    load(k_hbm, kv.at[0, 0], 0)
    load(v_hbm, kv.at[0, 1], 1)
    barrier = pltpu.get_barrier_semaphore()

    def greet(device):
        pl.semaphore_signal(barrier, inc=1, device_id=device, device_id_type=MESH)

    ahead = shifted(pick(-1 % inner_count, 2 % inner_count), 0)
    for device in (earlier(5), earlier(6), ahead, earlier(2, 4)):
        greet(device)
    greet(mate)
    load(lse_hbm, lse_ref, 2 + 3 * head_count)
    load(span_hbm, span_ref, 3 + 3 * head_count)
    load(code_hbm, code_ref, 4 + 3 * head_count)
    for h in range(head_count):
        columns = pl.ds(h * width, width)
        load(q_hbm.at[:, columns], q_vm.at[0, h], 2 + 3 * h)
        load(do_hbm.at[:, columns], do_vm.at[0, h], 3 + 3 * h)
        load(o_hbm.at[:, columns], o_vm.at[h], 4 + 3 * h)
    for copy in loads[:2]:
        copy.wait()

    pl.semaphore_wait(barrier, 5)

    def remote(src, dst, send_sem, recv_sem, device):
        return pltpu.make_async_remote_copy(
            src_ref=src, dst_ref=dst, send_sem=send_sem, recv_sem=recv_sem,
            device_id=device, device_id_type=MESH)

    def kv_copy(slot, device, source=0, to=None):
        to = slot if to is None else to
        return [remote(kv.at[source, part], kv.at[to, part], kv_send.at[slot - 1, part], kv_recv.at[to - 1, part], device)
                for part in range(2)]

    def wait_kv(slot, part):
        remote(kv.at[0, part], kv.at[slot, part], kv_send.at[slot - 1, part], kv_recv.at[slot - 1, part], mate).wait_recv()

    def begin(copies):
        for copy in copies:
            copy.start()

    def done(copies):
        for copy in copies:
            copy.wait_send()

    def pair_copy(src, dst, slot):
        return remote(src, dst, pair_send.at[slot], pair_recv.at[slot], mate)

    kv_sends = (kv_copy(pick(2, 1), later(2, 1)), kv_copy(6, later(6)), kv_copy(pick(4, 5), later(4, 5)))
    kv_even = kv_copy(5, later(5))
    relay = kv_copy(3, earlier(2), 5)
    @pl.when(outer_odd == 0)
    def _():
        begin(kv_sends[0])
        begin(kv_sends[1])

    for part in range(2):
        kv_sends[2][part].start()
        pl.when(is_even)(kv_even[part].start)

    @pl.when(outer_odd == 1)
    def _():
        begin(kv_sends[0])
        begin(kv_sends[1])

    for copy in loads[2:]:
        copy.wait()
    pairs = (pair_copy(q_vm.at[0], q_vm.at[1], 0), pair_copy(do_vm.at[0], do_vm.at[1], 1),
             pair_copy(meta.at[0], meta.at[1], 2))
    dq_pair = tuple(pair_copy(dq_out.at[at], dq_in.at[at], 3 + at) for at in range(2))
    pairs[0].start()
    pairs[1].start()
    meta[0, pl.ds(0, head_count), :] = lse_ref[...] * LOG2_E
    for h in range(head_count):
        product = do_vm[0, h].astype(jnp.float32) * o_vm[h].astype(jnp.float32)
        meta[0, pl.ds(head_count + h, 1), :] = jnp.sum(product.T, axis=0, keepdims=True)
    for at in range(steps - 1):
        meta[0, pl.ds(first_code + at, 1), :] = jnp.full((1, rows), code_ref[0, at].astype(jnp.float32))
    pairs[2].start()

    def g_copy(slot, part, device):
        return remote(g_out.at[slot - 1, part], g_in.at[slot - 1, part], g_send.at[slot - 1, part], g_recv.at[slot - 1, part], device)

    def position(device, shape, dim):
        u, w = device
        block = u * outer_count + w
        first, second = span_ref[2 * block], span_ref[2 * block + 1]
        at = lax.broadcasted_iota(jnp.int32, shape, dim)
        return jnp.where(at < half, first * half + at, second * half + at - half)

    features = head_count * rows

    def dot(x, y, dims):
        return lax.dot_general(x, y, (dims, ((), ())), preferred_element_type=jnp.float32)

    def reach(own, code_step):
        query_pos = position((inner_at, outer_at) if own == 0 else mate, (1, rows), 1)
        if code_step == 0:
            return query_pos
        row = first_code - 1 + (pick(5, 3) if code_step is None else code_step)
        code = meta[own, pl.ds(row, 1), :]
        limit = jnp.where(code == 2.0, jnp.int32(2 ** 31 - 1), jnp.int32(-1))
        return jnp.where(code == 1.0, query_pos, limit)

    def visit(slot, key_device, queries, arrive, give):
        arrive(0)
        key_block = kv[slot, 0]
        first, count = queries[0][0], len(queries)
        q_all = q_vm[pl.ds(first, count)].reshape(count * features, width)
        do_all = do_vm[pl.ds(first, count)].reshape(count * features, width)
        key_pos = position(key_device, (rows, rows), 0)
        allowed, lse_rows, delta_rows = [], [], []
        for own, code_step in queries:
            allowed += [key_pos <= reach(own, code_step)] * head_count
            lse_rows += [meta[own, pl.ds(h, 1), :] for h in range(head_count)]
            delta_rows += [meta[own, pl.ds(head_count + h, 1), :] for h in range(head_count)]
        allowed, lse_row, delta_row = (jnp.concatenate(x, axis=1) for x in (allowed, lse_rows, delta_rows))
        scores = dot(key_block, q_all, ((1,), (1,))) * (scale * LOG2_E)
        probs = jnp.where(allowed, jnp.exp2(scores - lse_row), 0.0)
        give(1, dot(probs.astype(jnp.bfloat16), do_all, ((1,), (0,))))
        arrive(1)
        dprob = dot(kv[slot, 1], do_all, ((1,), (1,)))
        dscore = (probs * (dprob - delta_row) * scale).astype(jnp.bfloat16)
        give(0, dot(dscore, q_all, ((1,), (0,))))
        query_part = dot(key_block.T, dscore, ((1,), (0,)))
        for at, (own, _) in enumerate(queries):
            dq_acc[own] += query_part[:, at * features:(at + 1) * features]

    def send_g(slot, device):
        def give(part, value):
            g_out[slot - 1, part] = value.astype(jnp.bfloat16)
            g_copy(slot, part, device).start()

        return give

    def come(slot):
        return lambda part: wait_kv(slot, part)

    def keep(part, value):
        own_acc[part] = value

    def add(part, value):
        own_acc[part] += value

    def nothing(part):
        pass

    dq_acc[...] = jnp.zeros_like(dq_acc)
    visit(0, (inner_at, outer_at), ((0, 0),), nothing, keep)
    for copy in pairs:
        copy.wait_recv()
    def send_dq():
        for at, copy in enumerate(dq_pair):
            dq_out[at] = dq_acc[1, :, pl.ds(at * features // 2, features // 2)].astype(jnp.bfloat16)
            copy.start()

    @pl.when(is_even)
    def _():
        visit(0, (inner_at, outer_at), ((1, 1),), nothing, add)
        visit(1, earlier(1), ((0, 1), (1, 2)), come(1), send_g(1, earlier(1)))
        send_dq()
        visit(2, earlier(2), ((0, 2),), come(2), send_g(2, earlier(2)))

    def last_step():
        visit(6, earlier(6), ((0, 6),), come(6), send_g(6, earlier(6)))

    pl.when(outer_odd == 0)(last_step)

    def hand_on(part):
        wait_kv(5, part)
        relay[part].start()

    @pl.when(is_odd)
    def _():
        visit(5, earlier(5), ((0, 5), (1, 4)), hand_on, send_g(5, earlier(5)))
        visit(4, earlier(4), ((0, 4), (1, 3)), come(4), send_g(4, earlier(4)))

    near = pick(5, 3)
    visit(near, earlier(5, 3), ((0, None),), come(near), send_g(near, earlier(5, 3)))
    pl.when(is_odd)(send_dq)
    pl.when(outer_odd == 1)(last_step)

    for h in range(head_count):
        at, place = divmod(h, head_count // 2)
        if place == 0:
            dq_pair[at].wait_recv()
        part = dq_in[at, :, pl.ds(place * rows, rows)].astype(jnp.float32)
        total = dq_acc[0, :, pl.ds(h * rows, rows)] + part
        dq_ref[:, pl.ds(h * width, width)] = total.T.astype(jnp.bfloat16)

    upper = pick(4, 3)
    last = (pick(2, 1), 6 - outer_odd, 5 + outer_odd * (upper - 5), upper + outer_odd * (6 - upper))
    for slot in last[:-1]:
        for part in (1, 0):
            g_copy(slot, part, mate).wait_recv()
        own_acc[...] += g_in[slot - 1].astype(jnp.float32)
    for part, out in ((1, dv_ref), (0, dk_ref)):
        g_copy(last[-1], part, mate).wait_recv()
        out[...] = (own_acc[part] + g_in[last[-1] - 1, part].astype(jnp.float32)).astype(jnp.bfloat16)

    for copy in pairs + dq_pair:
        copy.wait_send()
    for copies in kv_sends:
        done(copies)
    pl.when(is_even)(functools.partial(done, kv_even))
    pl.when(is_odd)(functools.partial(done, relay))
    for slot in (pick(1, 4), pick(2, 3), 5, 6):
        for part in range(2):
            g_copy(slot, part, mate).wait_send()


def finish(dq_in, dk_in, dv_in, dq_out, dk_out, dv_out, sems):
    moves = [pltpu.make_async_copy(src, dst, sems.at[slot])
             for slot, (src, dst) in enumerate(((dq_in, dq_out), (dk_in, dk_out), (dv_in, dv_out)))]
    for move in moves:
        move.start()
    for move in moves:
        move.wait()


def shards(queries, keys, values, out_grad, forward_out, log_sum_exp, span_table, mask_codes):
    rows, features = queries.shape
    width = keys.shape[1]
    heads = log_sum_exp.shape[0]
    remote = len(WINDOW_PATH) - 1
    hbm = pl.BlockSpec(memory_space=pl.ANY)
    vmem = pl.BlockSpec(memory_space=pltpu.VMEM)
    grads = (
        jax.ShapeDtypeStruct((rows, features), jnp.bfloat16),
        jax.ShapeDtypeStruct((rows, width), jnp.bfloat16),
        jax.ShapeDtypeStruct((rows, width), jnp.bfloat16),
    )
    parts = pl.pallas_call(
        functools.partial(kernel, lax.axis_size("inner"), lax.axis_size("outer")),
        out_shape=grads,
        in_specs=[hbm] * 8,
        out_specs=(vmem, vmem, vmem),
        scratch_shapes=[
            pltpu.VMEM((heads, rows), jnp.float32),
            pltpu.SMEM(span_table.shape, jnp.int32),
            pltpu.SMEM(mask_codes.shape, jnp.int32),
            pltpu.VMEM((2, heads, rows, width), jnp.bfloat16),
            pltpu.VMEM((2, heads, rows, width), jnp.bfloat16),
            pltpu.VMEM((heads, rows, width), jnp.bfloat16),
            pltpu.VMEM((2, 2 * heads + 8, rows), jnp.float32),
            pltpu.VMEM((1 + remote, 2, rows, width), jnp.bfloat16),
            pltpu.VMEM((remote, 2, rows, width), jnp.bfloat16),
            pltpu.VMEM((remote, 2, rows, width), jnp.bfloat16),
            pltpu.VMEM((2, width, heads * rows), jnp.float32),
            pltpu.VMEM((2, width, heads * rows // 2), jnp.bfloat16),
            pltpu.VMEM((2, width, heads * rows // 2), jnp.bfloat16),
            pltpu.VMEM((2, rows, width), jnp.float32),
            pltpu.SemaphoreType.DMA((5 + 3 * heads,)),
            pltpu.SemaphoreType.DMA((remote, 2)),
            pltpu.SemaphoreType.DMA((remote, 2)),
            pltpu.SemaphoreType.DMA((remote, 2)),
            pltpu.SemaphoreType.DMA((remote, 2)),
            pltpu.SemaphoreType.DMA((5,)),
            pltpu.SemaphoreType.DMA((5,)),
        ],
        compiler_params=pltpu.CompilerParams(
            collective_id=0, has_side_effects=True, vmem_limit_bytes=16 * 2 ** 20),
    )(*(pltpu.with_memory_space_constraint(x, pltpu.HBM) for x in (queries, keys, values, out_grad, forward_out, log_sum_exp, span_table, mask_codes)))
    return pl.pallas_call(
        finish,
        out_shape=grads,
        in_specs=[hbm] * 3,
        out_specs=(hbm, hbm, hbm),
        scratch_shapes=[pltpu.SemaphoreType.DMA((3,))],
        compiler_params=pltpu.CompilerParams(vmem_limit_bytes=2 ** 20),
    )(*parts)


def solution(mesh):
    return jax.shard_map(
        shards,
        mesh=mesh,
        in_specs=(
            P(("inner", "outer"), None),
            P(("inner", "outer"), None),
            P(("inner", "outer"), None),
            P(("inner", "outer"), None),
            P(("inner", "outer"), None),
            P(None, ("inner", "outer")),
            P(),
            P(("inner", "outer"), None),
        ),
        out_specs=(
            P(("inner", "outer"), None),
            P(("inner", "outer"), None),
            P(("inner", "outer"), None),
        ),
        check_vma=False,
    )
```
